256 devices in a mesh: gx: 16 (over z, core), gy: 16 (over x, y).
Axes of the slice: x: 4, y: 4, z: 8, core: 2. Of those that a mesh axis runs over, the one named last changes fastest.
Arguments:
- ref_pos: float32 [3, 131072], P(None, ('gx', 'gy')), as said below
- disp: float32 [3, 131072], P(None, ('gx', 'gy')), may hold values from -0.18 to 0.18
- volume: float32 [131072], P(('gx', 'gy')), may hold values from 0.6 to 1.4
- plastic: float32 [6, 131072], P(None, ('gx', 'gy')), may hold values from -0.06 to 0.06
- material: int32 [131072], P(('gx', 'gy')), may hold values from 0 to 2
- pair_list: int32 [256, 3, 26], P(('gx', 'gy')), may hold values from 0 to 8, as said below
- pair_count: int32 [256], P(('gx', 'gy')), may hold values from 6 to 22, as said below
Outputs:
- force: float32 [3, 131072], P(None, ('gx', 'gy'))
- plastic_new: float32 [6, 131072], P(None, ('gx', 'gy'))
The draws below stay inside these ranges and needn't reach their ends.
Inputs may be any that keep to these rules, and one draw needn't show every extreme that they name: `pair_list`: entries 0 to pair_count - 1 of a device's list name distinct pairs of blocks that touch in the plane (a king's move in the grid of blocks), its own block first; every such pair of different blocks appears in exactly one device's list, in the list of one of its two owners; every device lists some pair with each of the devices beside it along gx and along gy; entries from pair_count on are 0, 0, 4. Direction 4 is the device itself, and no entry names a device off the grid. `pair_count`: some device holds 22 live entries in every draw. `ref_pos`: particles sit within 0.3 of a lattice of unit spacing, 4 x 4 x 8 to a block, blocks of a device in a 2 x 2 grid, devices in the gx, gy grid.
All inputs are finite; a program needn't handle non-finite values.
Results may differ from the reference program's by a relative error of at most 0.00019.
Values sent between devices are 32-bit elements; how exact they have to be, the bound alone decides.
A program may use at most 64 MiB of HBM per device.

```python
import jax
import jax.numpy as jnp
import numpy as np
from jax import lax

BG = 2
BLOCK = 128
NB = 4
NPD = 512
NPART = 131072
PAIRS = 26
N_GX = 16
N_GY = 16
DEVICES = 256


def candidate_table(blocks_side):
    rows = []
    for block_x in range(blocks_side):
        for block_y in range(blocks_side):
            for step_x in (-1, 0, 1):
                for step_y in (-1, 0, 1):
                    if step_x == 0 and step_y == 0:
                        continue
                    other_x = block_x + step_x
                    other_y = block_y + step_y
                    dev_x = other_x // blocks_side if other_x >= 0 else -1
                    dev_y = other_y // blocks_side if other_y >= 0 else -1
                    local_x = other_x - dev_x * blocks_side
                    local_y = other_y - dev_y * blocks_side
                    if dev_x == 0 and dev_y == 0:
                        if (step_x, step_y) not in ((1, 0), (0, 1), (1, 1), (1, -1)):
                            continue
                    flipped = 0
                    if dev_x != 0 and dev_y == 0 and (step_y == 0) and (block_y == 0):
                        flipped = 1
                    if dev_y != 0 and dev_x == 0 and (step_x == 0) and (block_x == 0):
                        flipped = 1
                    rows.append([block_x * blocks_side + block_y, local_x * blocks_side + local_y, (dev_x + 1) * 3 + dev_y + 1, dev_x, dev_y, flipped])
    return np.asarray(rows, dtype=np.int32)


def pair_tables(key):
    center_key = jax.random.fold_in(key, 7)
    center_x = jax.random.randint(jax.random.fold_in(center_key, 1), (), 1, N_GX - 1)
    center_y = jax.random.randint(jax.random.fold_in(center_key, 2), (), 1, N_GY - 1)
    table = jnp.asarray(candidate_table(BG))
    device = jnp.arange(DEVICES, dtype=jnp.int32)
    grid_x = device // N_GY
    grid_y = device % N_GY
    near_x = grid_x[:, None] + table[None, :, 3]
    near_y = grid_y[:, None] + table[None, :, 4]
    inside = (near_x >= 0) & (near_x < N_GX) & (near_y >= 0) & (near_y < N_GY)
    internal = (table[None, :, 3] == 0) & (table[None, :, 4] == 0)
    mine = ((grid_x - center_x) ** 2 + (grid_y - center_y) ** 2)[:, None]
    theirs = (near_x - center_x) ** 2 + (near_y - center_y) ** 2
    neighbour = near_x * N_GY + near_y
    closer = (mine < theirs) | (mine == theirs) & (device[:, None] < neighbour)
    flipped = table[None, :, 5] == 1
    owned = internal | inside & (closer != flipped)
    score = jnp.where(owned, 0, PAIRS) + jnp.arange(PAIRS, dtype=jnp.int32)[None, :]
    order = jnp.argsort(score, axis=1)
    count = jnp.sum(owned.astype(jnp.int32), axis=1)
    live = jnp.arange(PAIRS, dtype=jnp.int32)[None, :] < count[:, None]
    first = jnp.where(live, table[:, 0][order], 0)
    second = jnp.where(live, table[:, 1][order], 0)
    where_dir = jnp.where(live, table[:, 2][order], 4)
    return (jnp.stack([first, second, where_dir], axis=1).astype(jnp.int32), count.astype(jnp.int32))


def draw_pair_list(key, part):
    return pair_tables(key)[0]


def draw_pair_count(key, part):
    return pair_tables(key)[1]


def draw_ref_pos(key, part):
    index = jnp.arange(NPART, dtype=jnp.int32)
    device = index // NPD
    local = index % NPD
    block = local // BLOCK
    inner = local % BLOCK
    grid_x = device // N_GY * BG + block // BG
    grid_y = device % N_GY * BG + block % BG
    lattice = jnp.stack([grid_x * 4 + inner // 32, grid_y * 4 + inner // 8 % 4, inner % 8]).astype(jnp.float32)
    jitter = jax.random.uniform(key, (3, NPART), jnp.float32, -0.2, 0.2)
    return lattice + jitter


def with_ends(array, key, smallest, high):
    place = [jax.random.randint(jax.random.fold_in(key, axis), (), 0, length) for axis, length in enumerate(array.shape)]
    main_axis = array.shape.index(max(array.shape))
    beside = place[:main_axis] + [(place[main_axis] + 1) % array.shape[main_axis]] + place[main_axis + 1:]
    return array.at[tuple(place)].set(smallest).at[tuple(beside)].set(high)


def levels(stream_key, shape, cuts, smallest, largest):
    level = 1.0
    for dim, parts in cuts:
        steps = jax.random.uniform(jax.random.fold_in(jax.random.fold_in(stream_key, 6), dim), (parts,), jnp.float32, smallest / len(cuts), largest / len(cuts))
        level = level * jnp.repeat(jnp.exp(steps), shape[dim] // parts).reshape((-1,) + (1,) * (len(shape) - 1 - dim))
    return level


def gaussian(stream_key, extent, scale, reach, pieces=(), held_as=jnp.bfloat16):
    entries = scale * jax.random.normal(stream_key, extent, jnp.float32)
    if pieces:
        entries = entries * levels(stream_key, extent, pieces, -0.22, 0.18)
    return jnp.clip(entries, -reach, reach).astype(held_as)


def setup_inputs(seed: int = 0) -> dict:
    streams_of = jax.random.split(jax.random.key(seed), 8)
    ref_pos = draw_ref_pos(jax.random.fold_in(streams_of[7], 71), 0)
    disp = gaussian(streams_of[1], (3, NPART), 0.03, 0.18, ((1, 256),), jnp.float32)
    volume = jnp.clip(0.6 + 0.79999995 * jax.random.uniform(streams_of[2], (NPART,), jnp.float32) ** levels(streams_of[2], (NPART,), ((0, 256),), -0.2, 0.2), 0.6, 1.4)
    plastic = gaussian(streams_of[3], (6, NPART), 0.01, 0.06, ((1, 256),), jnp.float32)
    material = with_ends(jax.random.randint(streams_of[4], (NPART,), 0, 3), jax.random.fold_in(streams_of[4], 1), 0, 2).astype(jnp.int32)
    pair_list = draw_pair_list(jax.random.fold_in(streams_of[7], 71), 0)
    pair_count = draw_pair_count(jax.random.fold_in(streams_of[7], 71), 0)
    return dict(ref_pos=ref_pos, disp=disp, volume=volume, plastic=plastic, material=material, pair_list=pair_list, pair_count=pair_count)


RADIUS = 2.0
KERNEL_SCALE = 1.5
REGULAR_SHIFT = 0.1
SHEAR_TABLE = (30.0, 40.0, 60.0)
BULK_TABLE = (60.0, 80.0, 120.0)
YIELD_TABLE = (1.0, 1.4, 2.2)
SYM_PAIRS = ((0, 0), (1, 1), (2, 2), (0, 1), (0, 2), (1, 2))

def kernel_parts(left, right):
    offset = right[0:3, None, :] - left[0:3, :, None]
    dist = jnp.sqrt(lax.optimization_barrier(jnp.sum(offset * offset, axis=0)))
    weight = KERNEL_SCALE * jnp.maximum(1.0 - dist / RADIUS, 0.0) ** 3
    return (offset, weight)

def moment_tile(left, right):
    offset, weight = kernel_parts(left, right)
    moved = offset + (right[3:6, None, :] - left[3:6, :, None])
    terms = [weight * offset[row_axis] * offset[col_axis] for row_axis, col_axis in SYM_PAIRS]
    terms = terms + [weight * moved[row_axis] * offset[col_axis] for row_axis in range(3) for col_axis in range(3)]
    terms = jnp.stack(terms)
    home = lax.optimization_barrier(jnp.sum(terms * right[6][None, None, :], axis=2))
    far = lax.optimization_barrier(jnp.sum(terms * left[6][None, :, None], axis=1))
    return (home, far)

def force_tile(left, right):
    offset, weight = kernel_parts(left, right)
    scaled = weight * left[6][:, None] * right[6][None, :]
    comps = []
    for row_axis in range(3):
        inner = 0.0
        for col_axis in range(3):
            entry = 7 + 3 * row_axis + col_axis
            inner = inner + (left[entry][:, None] + right[entry][None, :]) * offset[col_axis]
        comps.append(scaled * inner)
    terms = jnp.stack(comps)
    return (lax.optimization_barrier(jnp.sum(terms, axis=2)), -lax.optimization_barrier(jnp.sum(terms, axis=1)))

def constitutive(moments, plastic, material):
    m00 = moments[0] + REGULAR_SHIFT
    m11 = moments[1] + REGULAR_SHIFT
    m22 = moments[2] + REGULAR_SHIFT
    m01, m02, m12 = (moments[3], moments[4], moments[5])
    c00 = m11 * m22 - m12 * m12
    c01 = m02 * m12 - m01 * m22
    c02 = m01 * m12 - m02 * m11
    c11 = m00 * m22 - m02 * m02
    c12 = m01 * m02 - m00 * m12
    c22 = m00 * m11 - m01 * m01
    determ = m00 * c00 + m01 * c01 + m02 * c02
    correct = [[c00 / determ, c01 / determ, c02 / determ], [c01 / determ, c11 / determ, c12 / determ], [c02 / determ, c12 / determ, c22 / determ]]
    stretch = [[moments[6 + 3 * row_axis + col_axis] + (REGULAR_SHIFT if row_axis == col_axis else 0.0) for col_axis in range(3)] for row_axis in range(3)]
    grad = [[stretch[row_axis][0] * correct[0][col_axis] + stretch[row_axis][1] * correct[1][col_axis] + stretch[row_axis][2] * correct[2][col_axis] for col_axis in range(3)] for row_axis in range(3)]
    strain = []
    for index_sym, (row_axis, col_axis) in enumerate(SYM_PAIRS):
        value = 0.5 * (grad[row_axis][col_axis] + grad[col_axis][row_axis]) - plastic[index_sym]
        if row_axis == col_axis:
            value = value - 1.0
        strain.append(value)
    selector = (material[None, :] == jnp.arange(3, dtype=jnp.int32)[:, None]).astype(jnp.float32)
    shear = lax.optimization_barrier(jnp.sum(jnp.asarray(SHEAR_TABLE, jnp.float32)[:, None] * selector, axis=0))
    bulk = lax.optimization_barrier(jnp.sum(jnp.asarray(BULK_TABLE, jnp.float32)[:, None] * selector, axis=0))
    yield_stress = lax.optimization_barrier(jnp.sum(jnp.asarray(YIELD_TABLE, jnp.float32)[:, None] * selector, axis=0))
    trace_part = strain[0] + strain[1] + strain[2]
    deviator = [strain[index_sym] - (trace_part / 3.0 if index_sym < 3 else 0.0) for index_sym in range(6)]
    trial = [2.0 * shear * value for value in deviator]
    squares = trial[0] ** 2 + trial[1] ** 2 + trial[2] ** 2 + 2.0 * (trial[3] ** 2 + trial[4] ** 2 + trial[5] ** 2)
    equiv = jnp.sqrt(1.5 * squares)
    factor = yield_stress / jnp.maximum(equiv, yield_stress)
    plastic_new = jnp.stack([plastic[index_sym] + (1.0 - factor) * deviator[index_sym] for index_sym in range(6)])
    sym_stress = [factor * trial[index_sym] + (bulk * trace_part if index_sym < 3 else 0.0) for index_sym in range(6)]
    full = [[sym_stress[0], sym_stress[3], sym_stress[4]], [sym_stress[3], sym_stress[1], sym_stress[5]], [sym_stress[4], sym_stress[5], sym_stress[2]]]
    piola = jnp.stack([full[row_axis][0] * correct[0][col_axis] + full[row_axis][1] * correct[1][col_axis] + full[row_axis][2] * correct[2][col_axis] for row_axis in range(3) for col_axis in range(3)])
    return (piola, plastic_new)

def add_block(accum, value, block_index):
    current = lax.dynamic_index_in_dim(accum, block_index, 1, keepdims=False)
    return lax.dynamic_update_index_in_dim(accum, current + value, block_index, 1)

def accumulate(state, tile_fn, width, home_idx, far_idx, alive):
    nblk = state.shape[1]
    accum = jnp.zeros((width, nblk, BLOCK), jnp.float32)

    def pair_step(accum, item):
        first, second, keep = item
        left = lax.dynamic_index_in_dim(state, first, 1, keepdims=False)
        right = lax.dynamic_index_in_dim(state, second, 1, keepdims=False)
        home, far = tile_fn(left, right)
        accum = add_block(accum, home * keep, first)
        accum = add_block(accum, far * keep, second)
        return (accum, None)
    accum, _ = lax.scan(pair_step, accum, (home_idx, far_idx, alive))

    def self_step(accum, block_index):
        tile = lax.dynamic_index_in_dim(state, block_index, 1, keepdims=False)
        home, far = tile_fn(tile, tile)
        return (add_block(accum, home, block_index), None)
    accum, _ = lax.scan(self_step, accum, jnp.arange(nblk, dtype=jnp.int32))
    return accum.reshape(width, nblk * BLOCK)

def reference(ref_pos, disp, volume, plastic, material, pair_list, pair_count):
    nblk = DEVICES * NB
    state = jnp.concatenate([ref_pos, disp, volume[None, :]], axis=0).reshape(7, nblk, BLOCK)
    lists = jnp.transpose(pair_list, (1, 0, 2)).reshape(3, DEVICES * PAIRS).astype(jnp.int32)
    flat = jnp.arange(DEVICES * PAIRS, dtype=jnp.int32)
    devices = flat // PAIRS
    slots = flat % PAIRS
    alive = (slots < pair_count.astype(jnp.int32)[devices]).astype(jnp.float32)
    dirs = lists[2]
    far_dev = (devices // N_GY + dirs // 3 - 1) * N_GY + devices % N_GY + dirs % 3 - 1
    home_idx = (devices * NB + lists[0]).astype(jnp.int32)
    far_idx = (far_dev * NB + lists[1]).astype(jnp.int32)
    moments = accumulate(state, moment_tile, 15, home_idx, far_idx, alive)
    piola, plastic_new = constitutive(moments, plastic, material)
    state_two = jnp.concatenate([state.reshape(7, nblk * BLOCK), piola], axis=0).reshape(16, nblk, BLOCK)
    force = accumulate(state_two, force_tile, 3, home_idx, far_idx, alive)
    return (force, plastic_new)
```

```python
import functools

import jax
import jax.numpy as jnp
from jax import lax
from jax.experimental import pallas as pl
from jax.experimental.pallas import tpu as pltpu
from jax.sharding import PartitionSpec as P

BLOCK = 128
COMPS = 16
SHIFT = 0.1
SYM = ((0, 0), (1, 1), (2, 2), (0, 1), (0, 2), (1, 2))
DIRS = tuple((dx, dy) for dx in (-1, 0, 1) for dy in (-1, 0, 1) if (dx, dy) != (0, 0))
MESH = pl.DeviceIdType.MESH
F32 = jnp.float32


def exact_product(values, onehot, contract):
    high = values.astype(jnp.bfloat16)
    rest = values - high.astype(F32)
    mid = rest.astype(jnp.bfloat16)
    low = (rest - mid.astype(F32)).astype(jnp.bfloat16)
    parts = jnp.concatenate([high, mid, low], axis=0)
    out = lax.dot_general(parts, onehot, (((1,), (contract,)), ((), ())), preferred_element_type=F32)
    return out[0:16] + out[16:32] + out[32:48]


def send_range(step):
    if step == 0:
        return (1, 2), 1
    return ((2, 1), 0) if step == 1 else ((1, 1), 3)


def constitutive(moment, strain_sum, plastic, material):
    m00, m11, m22 = moment[0] + SHIFT, moment[1] + SHIFT, moment[2] + SHIFT
    m01, m02, m12 = moment[3:6]
    c00 = m11 * m22 - m12 * m12
    c01 = m02 * m12 - m01 * m22
    c02 = m01 * m12 - m02 * m11
    c11 = m00 * m22 - m02 * m02
    c12 = m01 * m02 - m00 * m12
    c22 = m00 * m11 - m01 * m01
    inverse = 1.0 / (m00 * c00 + m01 * c01 + m02 * c02)
    c00, c01, c02, c11, c12, c22 = [inverse * c for c in (c00, c01, c02, c11, c12, c22)]
    correct = [[c00, c01, c02], [c01, c11, c12], [c02, c12, c22]]
    grad = [
        [sum(strain_sum[3 * a + k] * correct[k][b] for k in range(3)) for b in range(3)]
        for a in range(3)
    ]
    strain = [0.5 * (grad[a][b] + grad[b][a]) - plastic[s] for s, (a, b) in enumerate(SYM)]
    first, second = material == 0.0, material == 1.0
    shear = jnp.where(first, 30.0, jnp.where(second, 40.0, 60.0))
    bulk = jnp.where(first, 60.0, jnp.where(second, 80.0, 120.0))
    yield_stress = jnp.where(first, 1.0, jnp.where(second, 1.4, 2.2))
    trace = strain[0] + strain[1] + strain[2]
    third = trace * (1.0 / 3.0)
    dev = [strain[s] - third if s < 3 else strain[s] for s in range(6)]
    trial = [2.0 * shear * value for value in dev]
    squares = (trial[0] ** 2 + trial[1] ** 2 + trial[2] ** 2) + 2.0 * (
        trial[3] ** 2 + trial[4] ** 2 + trial[5] ** 2
    )
    factor = yield_stress / jnp.maximum(jnp.sqrt(1.5 * squares), yield_stress)
    plastic_new = [plastic[s] + (1.0 - factor) * dev[s] for s in range(6)]
    pressure = bulk * trace
    s0, s1, s2, s3, s4, s5 = [
        factor * trial[s] + pressure if s < 3 else factor * trial[s] for s in range(6)
    ]
    full = [[s0, s3, s4], [s3, s1, s5], [s4, s5, s2]]
    piola = [
        full[a][0] * correct[0][b] + full[a][1] * correct[1][b] + full[a][2] * correct[2][b]
        for a in range(3)
        for b in range(3)
    ]
    return piola, plastic_new


def kernel(
    n_gx,
    n_gy,
    ref_ref,
    disp_ref,
    vol_ref,
    plastic_ref,
    material_ref,
    force_ref,
    plastic_out_ref,
    packed,
    onehots,
    region,
    state,
    rolled,
    weights,
    piolas,
    rolled_piolas,
    results,
    send_sem,
    recv_sem,
):
    gx = lax.axis_index("gx")
    gy = lax.axis_index("gy")

    def present(dx, dy):
        conditions = []
        if dx:
            conditions.append(gx < n_gx - 1 if dx > 0 else gx > 0)
        if dy:
            conditions.append(gy < n_gy - 1 if dy > 0 else gy > 0)
        return functools.reduce(jnp.logical_and, conditions)

    for rx in range(4):
        for ry in range(4):
            if rx in (0, 3) or ry in (0, 3):
                region[rx, ry] = jnp.zeros((COMPS, BLOCK), F32)

    barrier = pltpu.get_barrier_semaphore()
    for dx, dy in DIRS:

        @pl.when(present(dx, dy))
        def _():
            pl.semaphore_signal(
                barrier, inc=1, device_id={"gx": gx + dx, "gy": gy + dy}, device_id_type=MESH
            )

    row_index = lax.broadcasted_iota(jnp.int32, (BLOCK, BLOCK), 0).astype(F32)
    for block in range(4):
        lanes = pl.ds(block * BLOCK, BLOCK)
        packed[block, 0:3, :] = ref_ref[:, lanes]
        packed[block, 3:6, :] = disp_ref[:, lanes]
        packed[block, 6:7, :] = vol_ref[:, lanes]
        packed[block, 7:13, :] = plastic_ref[:, lanes]
        packed[block, 13:14, :] = material_ref[:, lanes].astype(F32)
        packed[block, 14:16, :] = jnp.zeros((2, BLOCK), F32)
        near = jnp.floor(ref_ref[:, lanes] + 0.5)
        near = near - jnp.min(near, axis=1, keepdims=True)
        site = near[0:1] * 32.0 + near[1:2] * 8.0 + near[2:3]
        onehot = jnp.where(row_index == site, 1.0, 0.0).astype(jnp.bfloat16)
        onehots[block] = onehot
        region[1 + block // 2, 1 + block % 2] = exact_product(packed[block], onehot, 1)

    beside = [
        1 + (place > 0).astype(jnp.int32) + (place < size - 1).astype(jnp.int32)
        for place, size in ((gx, n_gx), (gy, n_gy))
    ]
    pl.semaphore_wait(barrier, beside[0] * beside[1] - 1)

    def copy_to(number):
        dx, dy = DIRS[number]
        (sx, nx), tx = send_range(dx)
        (sy, ny), ty = send_range(dy)
        return pltpu.make_async_remote_copy(
            src_ref=region.at[pl.ds(sx, nx), pl.ds(sy, ny)],
            dst_ref=region.at[pl.ds(tx, nx), pl.ds(ty, ny)],
            send_sem=send_sem.at[number],
            recv_sem=recv_sem.at[number],
            device_id={"gx": gx + dx, "gy": gy + dy},
            device_id_type=MESH,
        )

    for number, (dx, dy) in enumerate(DIRS):

        @pl.when(present(dx, dy))
        def _():
            copy_to(number).start()

    for number, (dx, dy) in enumerate(DIRS):

        @pl.when(present(-dx, -dy))
        def _():
            copy_to(number).wait_recv()

    chunk = lax.broadcasted_iota(jnp.int32, (COMPS, BLOCK), 1) // 32
    for rx in range(4):
        blocks = [region[rx, ry] for ry in range(4)]
        for x in range(4):
            turned = [
                pltpu.roll(blocks[ry], 32 * (ry - x) % 128, 1) if ry != x else blocks[ry]
                for ry in range(4)
            ]
            low = jnp.where(chunk == 0, turned[0], turned[1])
            high = jnp.where(chunk == 2, turned[2], turned[3])
            value = jnp.where(chunk < 2, low, high)
            row = (rx * 4 + x + 4) % 16
            state[pl.ds(row, COMPS, stride=16), :] = value

    def piece(comp, part):
        return state[pl.ds(comp * 16 + part * 8, 8), :]

    z_lane = lax.broadcasted_iota(jnp.int32, (8, BLOCK), 1) % 8
    home = [[piece(c, part) for c in range(3)] for part in range(2)]

    def lane_shift(index):
        sy, sz = index // 5 - 2, index % 5 - 2
        return lax.rem(256 - (8 * sy + sz), 128), sz

    def moment_visit(index, sums):
        shift, sz = lane_shift(index)
        inside = (z_lane + sz >= 0) & (z_lane + sz < 8)
        reach = jnp.where(inside, 2.0, -100.0)
        for c in range(7):
            scale = 1.5 / 8.0 if c == 6 else None
            for part in range(2):
                value = piece(c, part)
                if scale is not None:
                    value = value * scale
                value = pltpu.roll(value, shift, 1)
                rolled[pl.ds(c * 32 + part * 8, 8), :] = value
                rolled[pl.ds(c * 32 + part * 8 + 16, 8), :] = value
        sums = [list(s) for s in sums]
        for sx in range(-2, 3):
            for part in range(2):
                base = 8 if part == 1 else 16
                other = [rolled[pl.ds(c * 32 + base + sx, 8), :] for c in range(7)]
                dX = [other[a] - home[part][a] for a in range(3)]
                square = dX[0] * dX[0] + dX[1] * dX[1] + dX[2] * dX[2]
                dist = square * lax.rsqrt(jnp.maximum(square, 1e-20))
                t = jnp.maximum(reach - dist, 0.0)
                w = (other[6] * t) * (t * t)
                g = [w * dX[a] for a in range(3)]
                acc = sums[part]
                for s, (a, b) in enumerate(SYM):
                    acc[s] = acc[s] + g[a] * dX[b]
                for a in range(3):
                    for b in range(3):
                        acc[6 + 3 * a + b] = acc[6 + 3 * a + b] + other[3 + a] * g[b]
                for a in range(3):
                    acc[15 + a] = acc[15 + a] + g[a]
                if part == 1:
                    for a in range(3):
                        weights[index, (sx + 2) * 3 + a] = g[a]
        return tuple(tuple(s) for s in sums)

    zero = jnp.zeros((8, BLOCK), F32)
    sums = lax.fori_loop(0, 25, moment_visit, tuple((zero,) * 18 for _ in range(2)))

    own_piola, own_plastic = None, None
    for part in range(2):
        acc = sums[part]
        disp = [piece(3 + a, part) for a in range(3)]
        strain_sum = [acc[6 + 3 * a + b] - disp[a] * acc[15 + b] for a in range(3) for b in range(3)]
        plastic = [piece(7 + s, part) for s in range(6)]
        piola, plastic_new = constitutive(acc[0:6], strain_sum, plastic, piece(13, part))
        for c in range(9):
            piolas[c, pl.ds(part * 8, 8), :] = piola[c]
        if part == 1:
            own_piola, own_plastic = piola, plastic_new
    for s in range(6):
        results[pl.ds((3 + s) * 8, 8), :] = own_plastic[s]
    lean = sums[1][15:18]
    start = tuple(sum(own_piola[3 * a + b] * lean[b] for b in range(3)) for a in range(3))

    def force_visit(index, force):
        shift, _ = lane_shift(index)
        for c in range(9):
            ring = pltpu.roll(piolas[c, 0:8, :], shift, 1)
            rolled_piolas[pl.ds(c * 24, 8), :] = ring
            rolled_piolas[pl.ds(c * 24 + 8, 8), :] = pltpu.roll(piolas[c, 8:16, :], shift, 1)
            rolled_piolas[pl.ds(c * 24 + 16, 8), :] = ring
        force = list(force)
        for sx in range(-2, 3):
            g = [weights[index, (sx + 2) * 3 + a] for a in range(3)]
            for a in range(3):
                for b in range(3):
                    other = rolled_piolas[pl.ds((3 * a + b) * 24 + 8 + sx, 8), :]
                    force[a] = force[a] + other * g[b]
        return tuple(force)

    force = lax.fori_loop(0, 25, force_visit, start)
    volume = piece(6, 1)
    for a in range(3):
        results[pl.ds(a * 8, 8), :] = volume * force[a]
    for c in range(9, 16):
        results[pl.ds(c * 8, 8), :] = zero

    for bx in range(2):
        rows = [results[pl.ds(bx * 4 + x, COMPS, stride=8), :] for x in range(4)]
        for by in range(2):
            block = bx * 2 + by
            turned = [pltpu.roll(rows[x], 32 * (x - by - 1) % 128, 1) for x in range(4)]
            low = jnp.where(chunk == 0, turned[0], turned[1])
            high = jnp.where(chunk == 2, turned[2], turned[3])
            value = exact_product(jnp.where(chunk < 2, low, high), onehots[block], 0)
            lanes = pl.ds(block * BLOCK, BLOCK)
            force_ref[:, lanes] = value[0:3]
            plastic_out_ref[:, lanes] = value[3:9]

    for number, (dx, dy) in enumerate(DIRS):

        @pl.when(present(dx, dy))
        def _():
            copy_to(number).wait_send()


def solution(mesh):
    n_gx, n_gy = mesh.shape["gx"], mesh.shape["gy"]

    def on_device(ref_pos, disp, volume, plastic, material, pair_list, pair_count):
        count = ref_pos.shape[1]
        vmem = pl.BlockSpec(memory_space=pltpu.VMEM)
        return pl.pallas_call(
            functools.partial(kernel, n_gx, n_gy),
            out_shape=(
                jax.ShapeDtypeStruct((3, count), F32),
                jax.ShapeDtypeStruct((6, count), F32),
            ),
            in_specs=[vmem] * 5,
            out_specs=(vmem, vmem),
            scratch_shapes=[
                pltpu.VMEM((4, COMPS, BLOCK), F32),
                pltpu.VMEM((4, BLOCK, BLOCK), jnp.bfloat16),
                pltpu.VMEM((4, 4, COMPS, BLOCK), F32),
                pltpu.VMEM((COMPS * 16, BLOCK), F32),
                pltpu.VMEM((7 * 32, BLOCK), F32),
                pltpu.VMEM((25, 15, 8, BLOCK), F32),
                pltpu.VMEM((9, 16, BLOCK), F32),
                pltpu.VMEM((9 * 24, BLOCK), F32),
                pltpu.VMEM((COMPS * 8, BLOCK), F32),
                pltpu.SemaphoreType.DMA((8,)),
                pltpu.SemaphoreType.DMA((8,)),
            ],
            compiler_params=pltpu.CompilerParams(collective_id=0, has_side_effects=True),
        )(ref_pos, disp, volume.reshape(1, count), plastic, material.reshape(1, count))

    in_specs = (
        P(None, ("gx", "gy")),
        P(None, ("gx", "gy")),
        P(("gx", "gy")),
        P(None, ("gx", "gy")),
        P(("gx", "gy")),
        P(("gx", "gy"), None, None),
        P(("gx", "gy")),
    )
    out_specs = (P(None, ("gx", "gy")), P(None, ("gx", "gy")))
    return jax.shard_map(
        on_device, mesh=mesh, in_specs=in_specs, out_specs=out_specs, check_vma=False
    )
```

```python
import functools

import jax
import jax.numpy as jnp
from jax import lax
from jax.experimental import pallas as pl
from jax.experimental.pallas import tpu as pltpu
from jax.sharding import PartitionSpec as P

BLOCK = 128
COMPS = 16
SHIFT = 0.1
SYM = ((0, 0), (1, 1), (2, 2), (0, 1), (0, 2), (1, 2))
DIRS = tuple((dx, dy) for dx in (-1, 0, 1) for dy in (-1, 0, 1) if (dx, dy) != (0, 0))
MESH = pl.DeviceIdType.MESH


def within_reach(sx, sy, sz):
    return sum(max(abs(step) - 0.6, 0.0) ** 2 for step in (sx, sy, sz)) < 4.0


STEPS = range(-2, 3)
OFFSETS = tuple(
    (sy, sz, tuple(sx for sx in STEPS if within_reach(sx, sy, sz))) for sy in STEPS for sz in STEPS
)
F32 = jnp.float32


def exact_product(values, onehot, contract):
    high = values.astype(jnp.bfloat16)
    rest = values - high.astype(F32)
    mid = rest.astype(jnp.bfloat16)
    low = (rest - mid.astype(F32)).astype(jnp.bfloat16)
    parts = jnp.concatenate([high, mid, low], axis=0)
    out = lax.dot_general(parts, onehot, (((1,), (contract,)), ((), ())), preferred_element_type=F32)
    return out[0:16] + out[16:32] + out[32:48]


def send_range(step):
    if step == 0:
        return (1, 2), 1
    return ((2, 1), 0) if step == 1 else ((1, 1), 3)


def constitutive(moment, strain_sum, plastic, material):
    m00, m11, m22 = moment[0] + SHIFT, moment[1] + SHIFT, moment[2] + SHIFT
    m01, m02, m12 = moment[3:6]
    c00 = m11 * m22 - m12 * m12
    c01 = m02 * m12 - m01 * m22
    c02 = m01 * m12 - m02 * m11
    c11 = m00 * m22 - m02 * m02
    c12 = m01 * m02 - m00 * m12
    c22 = m00 * m11 - m01 * m01
    inverse = 1.0 / (m00 * c00 + m01 * c01 + m02 * c02)
    c00, c01, c02, c11, c12, c22 = [inverse * c for c in (c00, c01, c02, c11, c12, c22)]
    correct = [[c00, c01, c02], [c01, c11, c12], [c02, c12, c22]]
    grad = [
        [sum(strain_sum[3 * a + k] * correct[k][b] for k in range(3)) for b in range(3)]
        for a in range(3)
    ]
    strain = [0.5 * (grad[a][b] + grad[b][a]) - plastic[s] for s, (a, b) in enumerate(SYM)]
    first, second = material == 0.0, material == 1.0
    shear = jnp.where(first, 30.0, jnp.where(second, 40.0, 60.0))
    bulk = jnp.where(first, 60.0, jnp.where(second, 80.0, 120.0))
    yield_stress = jnp.where(first, 1.0, jnp.where(second, 1.4, 2.2))
    trace = strain[0] + strain[1] + strain[2]
    third = trace * (1.0 / 3.0)
    dev = [strain[s] - third if s < 3 else strain[s] for s in range(6)]
    trial = [2.0 * shear * value for value in dev]
    squares = (trial[0] ** 2 + trial[1] ** 2 + trial[2] ** 2) + 2.0 * (
        trial[3] ** 2 + trial[4] ** 2 + trial[5] ** 2
    )
    factor = yield_stress / jnp.maximum(jnp.sqrt(1.5 * squares), yield_stress)
    plastic_new = [plastic[s] + (1.0 - factor) * dev[s] for s in range(6)]
    pressure = bulk * trace
    s0, s1, s2, s3, s4, s5 = [
        factor * trial[s] + pressure if s < 3 else factor * trial[s] for s in range(6)
    ]
    full = [[s0, s3, s4], [s3, s1, s5], [s4, s5, s2]]
    piola = [
        full[a][0] * correct[0][b] + full[a][1] * correct[1][b] + full[a][2] * correct[2][b]
        for a in range(3)
        for b in range(3)
    ]
    return piola, plastic_new


def kernel(
    n_gx,
    n_gy,
    ref_ref,
    disp_ref,
    vol_ref,
    plastic_ref,
    material_ref,
    force_ref,
    plastic_out_ref,
    packed,
    onehots,
    region,
    state,
    rolled,
    weights,
    piolas,
    rolled_piolas,
    results,
    send_sem,
    recv_sem,
):
    gx = lax.axis_index("gx")
    gy = lax.axis_index("gy")

    def present(dx, dy):
        conditions = []
        if dx:
            conditions.append(gx < n_gx - 1 if dx > 0 else gx > 0)
        if dy:
            conditions.append(gy < n_gy - 1 if dy > 0 else gy > 0)
        return functools.reduce(jnp.logical_and, conditions)

    for rx in range(4):
        for ry in range(4):
            if rx in (0, 3) or ry in (0, 3):
                region[rx, ry] = jnp.zeros((COMPS, BLOCK), F32)

    barrier = pltpu.get_barrier_semaphore()
    for dx, dy in DIRS:

        @pl.when(present(dx, dy))
        def _():
            pl.semaphore_signal(
                barrier, inc=1, device_id={"gx": gx + dx, "gy": gy + dy}, device_id_type=MESH
            )

    row_index = lax.broadcasted_iota(jnp.int32, (BLOCK, BLOCK), 0).astype(F32)
    for block in range(4):
        lanes = pl.ds(block * BLOCK, BLOCK)
        packed[block, 0:3, :] = ref_ref[:, lanes]
        packed[block, 3:6, :] = disp_ref[:, lanes]
        packed[block, 6:7, :] = vol_ref[:, lanes]
        packed[block, 7:13, :] = plastic_ref[:, lanes]
        packed[block, 13:14, :] = material_ref[:, lanes].astype(F32)
        packed[block, 14:16, :] = jnp.zeros((2, BLOCK), F32)
        near = jnp.floor(ref_ref[:, lanes] + 0.5)
        near = near - jnp.min(near, axis=1, keepdims=True)
        site = near[0:1] * 32.0 + near[1:2] * 8.0 + near[2:3]
        onehot = jnp.where(row_index == site, 1.0, 0.0).astype(jnp.bfloat16)
        onehots[block] = onehot
        region[1 + block // 2, 1 + block % 2] = exact_product(packed[block], onehot, 1)

    beside = [
        1 + (place > 0).astype(jnp.int32) + (place < size - 1).astype(jnp.int32)
        for place, size in ((gx, n_gx), (gy, n_gy))
    ]
    pl.semaphore_wait(barrier, beside[0] * beside[1] - 1)

    def copy_to(number):
        dx, dy = DIRS[number]
        (sx, nx), tx = send_range(dx)
        (sy, ny), ty = send_range(dy)
        return pltpu.make_async_remote_copy(
            src_ref=region.at[pl.ds(sx, nx), pl.ds(sy, ny)],
            dst_ref=region.at[pl.ds(tx, nx), pl.ds(ty, ny)],
            send_sem=send_sem.at[number],
            recv_sem=recv_sem.at[number],
            device_id={"gx": gx + dx, "gy": gy + dy},
            device_id_type=MESH,
        )

    for number, (dx, dy) in enumerate(DIRS):

        @pl.when(present(dx, dy))
        def _():
            copy_to(number).start()

    for number, (dx, dy) in enumerate(DIRS):

        @pl.when(present(-dx, -dy))
        def _():
            copy_to(number).wait_recv()

    chunk = lax.broadcasted_iota(jnp.int32, (COMPS, BLOCK), 1) // 32
    for rx in range(4):
        blocks = [region[rx, ry] for ry in range(4)]
        for x in range(4):
            turned = [
                pltpu.roll(blocks[ry], 32 * (ry - x) % 128, 1) if ry != x else blocks[ry]
                for ry in range(4)
            ]
            low = jnp.where(chunk == 0, turned[0], turned[1])
            high = jnp.where(chunk == 2, turned[2], turned[3])
            value = jnp.where(chunk < 2, low, high)
            row = (rx * 4 + x + 4) % 16
            state[pl.ds(row, COMPS, stride=16), :] = value

    def piece(comp, part):
        return state[pl.ds(comp * 16 + part * 8, 8), :]

    z_lane = lax.broadcasted_iota(jnp.int32, (8, BLOCK), 1) % 8
    home = [[piece(c, part) for c in range(3)] for part in range(2)]

    def moment_visit(slot, sy, sz, x_steps, sums):
        shift = -(8 * sy + sz) % 128
        inside = (z_lane + sz >= 0) & (z_lane + sz < 8)
        reach = jnp.where(inside, 2.0, -100.0)
        for c in range(7):
            for part in range(2):
                value = scaled[part] if c == 6 else piece(c, part)
                if shift:
                    value = pltpu.roll(value, shift, 1)
                rolled[slot, pl.ds(c * 32 + part * 8, 8), :] = value
                rolled[slot, pl.ds(c * 32 + part * 8 + 16, 8), :] = value
        for sx in x_steps:
            if (sx, sy, sz) == (0, 0, 0):
                continue
            for part in range(2):
                base = 8 if part == 1 else 16
                other = [rolled[slot, pl.ds(c * 32 + base + sx, 8), :] for c in range(7)]
                dX = [other[a] - home[part][a] for a in range(3)]
                square = dX[0] * dX[0] + dX[1] * dX[1] + dX[2] * dX[2]
                dist = square * lax.rsqrt(jnp.maximum(square, 1e-20))
                t = jnp.maximum(reach - dist, 0.0)
                w = (other[6] * t) * (t * t)
                g = [w * dX[a] for a in range(3)]
                acc = sums[part]
                for s, (a, b) in enumerate(SYM):
                    acc[s] = acc[s] + g[a] * dX[b]
                for a in range(3):
                    for b in range(3):
                        acc[6 + 3 * a + b] = acc[6 + 3 * a + b] + other[3 + a] * g[b]
                for a in range(3):
                    acc[15 + a] = acc[15 + a] + g[a]
                if part == 1:
                    for a in range(3):
                        weights[slot, (sx + 2) * 3 + a] = g[a]

    zero = jnp.zeros((8, BLOCK), F32)
    scaled = [piece(6, part) * (1.5 / 8.0) for part in range(2)]
    sums = [[zero] * 18 for _ in range(2)]
    for slot, (sy, sz, x_steps) in enumerate(OFFSETS):
        moment_visit(slot, sy, sz, x_steps, sums)

    own_piola, own_plastic = None, None
    for part in range(2):
        acc = sums[part]
        disp = [piece(3 + a, part) for a in range(3)]
        strain_sum = [acc[6 + 3 * a + b] - disp[a] * acc[15 + b] for a in range(3) for b in range(3)]
        plastic = [piece(7 + s, part) for s in range(6)]
        piola, plastic_new = constitutive(acc[0:6], strain_sum, plastic, piece(13, part))
        for c in range(9):
            piolas[c, pl.ds(part * 8, 8), :] = piola[c]
        if part == 1:
            own_piola, own_plastic = piola, plastic_new
    for s in range(6):
        results[pl.ds((3 + s) * 8, 8), :] = own_plastic[s]
    lean = sums[1][15:18]
    force = [sum(own_piola[3 * a + b] * lean[b] for b in range(3)) for a in range(3)]

    for slot, (sy, sz, x_steps) in enumerate(OFFSETS):
        shift = -(8 * sy + sz) % 128
        for c in range(9):
            ring, inner = piolas[c, 0:8, :], piolas[c, 8:16, :]
            if shift:
                ring, inner = pltpu.roll(ring, shift, 1), pltpu.roll(inner, shift, 1)
            rolled_piolas[slot, pl.ds(c * 24, 8), :] = ring
            rolled_piolas[slot, pl.ds(c * 24 + 8, 8), :] = inner
            rolled_piolas[slot, pl.ds(c * 24 + 16, 8), :] = ring
        for sx in x_steps:
            if (sx, sy, sz) == (0, 0, 0):
                continue
            g = [weights[slot, (sx + 2) * 3 + a] for a in range(3)]
            for a in range(3):
                for b in range(3):
                    other = rolled_piolas[slot, pl.ds((3 * a + b) * 24 + 8 + sx, 8), :]
                    force[a] = force[a] + other * g[b]

    volume = piece(6, 1)
    for a in range(3):
        results[pl.ds(a * 8, 8), :] = volume * force[a]
    for c in range(9, 16):
        results[pl.ds(c * 8, 8), :] = zero

    for bx in range(2):
        rows = [results[pl.ds(bx * 4 + x, COMPS, stride=8), :] for x in range(4)]
        for by in range(2):
            block = bx * 2 + by
            turned = [pltpu.roll(rows[x], 32 * (x - by - 1) % 128, 1) for x in range(4)]
            low = jnp.where(chunk == 0, turned[0], turned[1])
            high = jnp.where(chunk == 2, turned[2], turned[3])
            value = exact_product(jnp.where(chunk < 2, low, high), onehots[block], 0)
            lanes = pl.ds(block * BLOCK, BLOCK)
            force_ref[:, lanes] = value[0:3]
            plastic_out_ref[:, lanes] = value[3:9]

    for number, (dx, dy) in enumerate(DIRS):

        @pl.when(present(dx, dy))
        def _():
            copy_to(number).wait_send()


def solution(mesh):
    n_gx, n_gy = mesh.shape["gx"], mesh.shape["gy"]

    def on_device(ref_pos, disp, volume, plastic, material, pair_list, pair_count):
        count = ref_pos.shape[1]
        vmem = pl.BlockSpec(memory_space=pltpu.VMEM)
        return pl.pallas_call(
            functools.partial(kernel, n_gx, n_gy),
            out_shape=(
                jax.ShapeDtypeStruct((3, count), F32),
                jax.ShapeDtypeStruct((6, count), F32),
            ),
            in_specs=[vmem] * 5,
            out_specs=(vmem, vmem),
            scratch_shapes=[
                pltpu.VMEM((4, COMPS, BLOCK), F32),
                pltpu.VMEM((4, BLOCK, BLOCK), jnp.bfloat16),
                pltpu.VMEM((4, 4, COMPS, BLOCK), F32),
                pltpu.VMEM((COMPS * 16, BLOCK), F32),
                pltpu.VMEM((25, 7 * 32, BLOCK), F32),
                pltpu.VMEM((25, 15, 8, BLOCK), F32),
                pltpu.VMEM((9, 16, BLOCK), F32),
                pltpu.VMEM((25, 9 * 24, BLOCK), F32),
                pltpu.VMEM((COMPS * 8, BLOCK), F32),
                pltpu.SemaphoreType.DMA((8,)),
                pltpu.SemaphoreType.DMA((8,)),
            ],
            compiler_params=pltpu.CompilerParams(collective_id=0, has_side_effects=True),
        )(ref_pos, disp, volume.reshape(1, count), plastic, material.reshape(1, count))

    in_specs = (
        P(None, ("gx", "gy")),
        P(None, ("gx", "gy")),
        P(("gx", "gy")),
        P(None, ("gx", "gy")),
        P(("gx", "gy")),
        P(("gx", "gy"), None, None),
        P(("gx", "gy")),
    )
    out_specs = (P(None, ("gx", "gy")), P(None, ("gx", "gy")))
    return jax.shard_map(
        on_device, mesh=mesh, in_specs=in_specs, out_specs=out_specs, check_vma=False
    )
```

```python
import functools

import jax
import jax.numpy as jnp
from jax import lax
from jax.experimental import pallas as pl
from jax.experimental.pallas import tpu as pltpu
from jax.sharding import PartitionSpec as P

BLOCK = 128
COMPS = 16
SHIFT = 0.1
SYM = ((0, 0), (1, 1), (2, 2), (0, 1), (0, 2), (1, 2))
DIRS = tuple((dx, dy) for dx in (-1, 0, 1) for dy in (-1, 0, 1) if (dx, dy) != (0, 0))
MESH = pl.DeviceIdType.MESH


def within_reach(sx, sy, sz):
    return sum(max(abs(step) - 0.6, 0.0) ** 2 for step in (sx, sy, sz)) < 4.0


STEPS = range(-2, 3)
OFFSETS = tuple(
    (sy, sz, tuple(sx for sx in STEPS if within_reach(sx, sy, sz))) for sy in STEPS for sz in STEPS
)
F32 = jnp.float32


def exact_product(values, onehot, contract):
    high = values.astype(jnp.bfloat16)
    rest = values - high.astype(F32)
    mid = rest.astype(jnp.bfloat16)
    low = (rest - mid.astype(F32)).astype(jnp.bfloat16)
    parts = jnp.concatenate([high, mid, low], axis=0)
    out = lax.dot_general(parts, onehot, (((1,), (contract,)), ((), ())), preferred_element_type=F32)
    return out[0:16] + out[16:32] + out[32:48]


def send_range(step):
    if step == 0:
        return (1, 2), 1
    return ((2, 1), 0) if step == 1 else ((1, 1), 3)


def constitutive(moment, strain_sum, plastic, material):
    m00, m11, m22 = moment[0] + SHIFT, moment[1] + SHIFT, moment[2] + SHIFT
    m01, m02, m12 = moment[3:6]
    c00 = m11 * m22 - m12 * m12
    c01 = m02 * m12 - m01 * m22
    c02 = m01 * m12 - m02 * m11
    c11 = m00 * m22 - m02 * m02
    c12 = m01 * m02 - m00 * m12
    c22 = m00 * m11 - m01 * m01
    inverse = 1.0 / (m00 * c00 + m01 * c01 + m02 * c02)
    c00, c01, c02, c11, c12, c22 = [inverse * c for c in (c00, c01, c02, c11, c12, c22)]
    correct = [[c00, c01, c02], [c01, c11, c12], [c02, c12, c22]]
    grad = [
        [sum(strain_sum[3 * a + k] * correct[k][b] for k in range(3)) for b in range(3)]
        for a in range(3)
    ]
    strain = [0.5 * (grad[a][b] + grad[b][a]) - plastic[s] for s, (a, b) in enumerate(SYM)]
    first, second = material == 0.0, material == 1.0
    shear = jnp.where(first, 30.0, jnp.where(second, 40.0, 60.0))
    bulk = jnp.where(first, 60.0, jnp.where(second, 80.0, 120.0))
    yield_stress = jnp.where(first, 1.0, jnp.where(second, 1.4, 2.2))
    trace = strain[0] + strain[1] + strain[2]
    third = trace * (1.0 / 3.0)
    dev = [strain[s] - third if s < 3 else strain[s] for s in range(6)]
    trial = [2.0 * shear * value for value in dev]
    squares = (trial[0] ** 2 + trial[1] ** 2 + trial[2] ** 2) + 2.0 * (
        trial[3] ** 2 + trial[4] ** 2 + trial[5] ** 2
    )
    factor = yield_stress / jnp.maximum(jnp.sqrt(1.5 * squares), yield_stress)
    plastic_new = [plastic[s] + (1.0 - factor) * dev[s] for s in range(6)]
    pressure = bulk * trace
    s0, s1, s2, s3, s4, s5 = [
        factor * trial[s] + pressure if s < 3 else factor * trial[s] for s in range(6)
    ]
    full = [[s0, s3, s4], [s3, s1, s5], [s4, s5, s2]]
    piola = [
        full[a][0] * correct[0][b] + full[a][1] * correct[1][b] + full[a][2] * correct[2][b]
        for a in range(3)
        for b in range(3)
    ]
    return piola, plastic_new


def exchange_kernel(
    n_gx,
    n_gy,
    ref_hbm,
    disp_hbm,
    vol_hbm,
    plastic_hbm,
    material_hbm,
    region,
    onehots,
    ref_ref,
    disp_ref,
    vol_ref,
    plastic_ref,
    material_ref,
    packed,
    load_sem,
    send_sem,
    recv_sem,
):
    loads = [
        pltpu.make_async_copy(source, target, load_sem.at[number])
        for number, (source, target) in enumerate(
            (
                (ref_hbm, ref_ref),
                (disp_hbm, disp_ref),
                (vol_hbm, vol_ref),
                (plastic_hbm, plastic_ref),
                (material_hbm, material_ref),
            )
        )
    ]
    for load in loads:
        load.start()
    gx = lax.axis_index("gx")
    gy = lax.axis_index("gy")

    def present(dx, dy):
        conditions = []
        if dx:
            conditions.append(gx < n_gx - 1 if dx > 0 else gx > 0)
        if dy:
            conditions.append(gy < n_gy - 1 if dy > 0 else gy > 0)
        return functools.reduce(jnp.logical_and, conditions)

    for rx in range(4):
        for ry in range(4):
            if rx in (0, 3) or ry in (0, 3):
                region[rx, ry] = jnp.zeros((COMPS, BLOCK), F32)

    barrier = pltpu.get_barrier_semaphore()
    for dx, dy in DIRS:

        @pl.when(present(dx, dy))
        def _():
            pl.semaphore_signal(
                barrier, inc=1, device_id={"gx": gx + dx, "gy": gy + dy}, device_id_type=MESH
            )

    for load in loads:
        load.wait()

    row_index = lax.broadcasted_iota(jnp.int32, (BLOCK, BLOCK), 0).astype(F32)
    for block in range(4):
        lanes = pl.ds(block * BLOCK, BLOCK)
        packed[block, 0:3, :] = ref_ref[:, lanes]
        packed[block, 3:6, :] = disp_ref[:, lanes]
        packed[block, 6:7, :] = vol_ref[:, lanes]
        packed[block, 7:13, :] = plastic_ref[:, lanes]
        packed[block, 13:14, :] = material_ref[:, lanes].astype(F32)
        packed[block, 14:16, :] = jnp.zeros((2, BLOCK), F32)
        near = jnp.floor(ref_ref[:, lanes] + 0.5)
        near = near - jnp.min(near, axis=1, keepdims=True)
        site = near[0:1] * 32.0 + near[1:2] * 8.0 + near[2:3]
        onehot = jnp.where(row_index == site, 1.0, 0.0).astype(jnp.bfloat16)
        onehots[block] = onehot
        region[1 + block // 2, 1 + block % 2] = exact_product(packed[block], onehot, 1)

    beside = [
        1 + (place > 0).astype(jnp.int32) + (place < size - 1).astype(jnp.int32)
        for place, size in ((gx, n_gx), (gy, n_gy))
    ]
    pl.semaphore_wait(barrier, beside[0] * beside[1] - 1)

    def copy_to(number):
        dx, dy = DIRS[number]
        (sx, nx), tx = send_range(dx)
        (sy, ny), ty = send_range(dy)
        return pltpu.make_async_remote_copy(
            src_ref=region.at[pl.ds(sx, nx), pl.ds(sy, ny)],
            dst_ref=region.at[pl.ds(tx, nx), pl.ds(ty, ny)],
            send_sem=send_sem.at[number],
            recv_sem=recv_sem.at[number],
            device_id={"gx": gx + dx, "gy": gy + dy},
            device_id_type=MESH,
        )

    for number, (dx, dy) in enumerate(DIRS):

        @pl.when(present(dx, dy))
        def _():
            copy_to(number).start()

    for number, (dx, dy) in enumerate(DIRS):

        @pl.when(present(-dx, -dy))
        def _():
            copy_to(number).wait_recv()

    for number, (dx, dy) in enumerate(DIRS):

        @pl.when(present(dx, dy))
        def _():
            copy_to(number).wait_send()


def stencil_kernel(
    region,
    onehots,
    force_ref,
    plastic_out_ref,
    state,
    rolled,
    weights,
    piolas,
    rolled_piolas,
    results,
):
    chunk = lax.broadcasted_iota(jnp.int32, (COMPS, BLOCK), 1) // 32
    for rx in range(4):
        blocks = [region[rx, ry] for ry in range(4)]
        for x in range(4):
            turned = [
                pltpu.roll(blocks[ry], 32 * (ry - x) % 128, 1) if ry != x else blocks[ry]
                for ry in range(4)
            ]
            low = jnp.where(chunk == 0, turned[0], turned[1])
            high = jnp.where(chunk == 2, turned[2], turned[3])
            value = jnp.where(chunk < 2, low, high)
            row = (rx * 4 + x + 4) % 16
            state[pl.ds(row, COMPS, stride=16), :] = value

    def piece(comp, part):
        return state[pl.ds(comp * 16 + part * 8, 8), :]

    z_lane = lax.broadcasted_iota(jnp.int32, (8, BLOCK), 1) % 8
    home = [[piece(c, part) for c in range(3)] for part in range(2)]

    def moment_visit(slot, sy, sz, x_steps, sums):
        shift = -(8 * sy + sz) % 128
        inside = (z_lane + sz >= 0) & (z_lane + sz < 8)
        reach = jnp.where(inside, 2.0, -100.0)
        for c in range(7):
            for part in range(2):
                value = scaled[part] if c == 6 else piece(c, part)
                if shift:
                    value = pltpu.roll(value, shift, 1)
                rolled[slot, pl.ds(c * 32 + part * 8, 8), :] = value
                rolled[slot, pl.ds(c * 32 + part * 8 + 16, 8), :] = value
        for sx in x_steps:
            if (sx, sy, sz) == (0, 0, 0):
                continue
            for part in range(2):
                base = 8 if part == 1 else 16
                other = [rolled[slot, pl.ds(c * 32 + base + sx, 8), :] for c in range(7)]
                dX = [other[a] - home[part][a] for a in range(3)]
                square = dX[0] * dX[0] + dX[1] * dX[1] + dX[2] * dX[2]
                dist = square * lax.rsqrt(jnp.maximum(square, 1e-20))
                t = jnp.maximum(reach - dist, 0.0)
                w = (other[6] * t) * (t * t)
                g = [w * dX[a] for a in range(3)]
                acc = sums[part]
                for s, (a, b) in enumerate(SYM):
                    acc[s] = acc[s] + g[a] * dX[b]
                for a in range(3):
                    for b in range(3):
                        acc[6 + 3 * a + b] = acc[6 + 3 * a + b] + other[3 + a] * g[b]
                for a in range(3):
                    acc[15 + a] = acc[15 + a] + g[a]
                if part == 1:
                    for a in range(3):
                        weights[slot, (sx + 2) * 3 + a] = g[a]

    zero = jnp.zeros((8, BLOCK), F32)
    scaled = [piece(6, part) * (1.5 / 8.0) for part in range(2)]
    sums = [[zero] * 18 for _ in range(2)]
    for slot, (sy, sz, x_steps) in enumerate(OFFSETS):
        moment_visit(slot, sy, sz, x_steps, sums)

    own_piola, own_plastic = None, None
    for part in range(2):
        acc = sums[part]
        disp = [piece(3 + a, part) for a in range(3)]
        strain_sum = [acc[6 + 3 * a + b] - disp[a] * acc[15 + b] for a in range(3) for b in range(3)]
        plastic = [piece(7 + s, part) for s in range(6)]
        piola, plastic_new = constitutive(acc[0:6], strain_sum, plastic, piece(13, part))
        for c in range(9):
            piolas[c, pl.ds(part * 8, 8), :] = piola[c]
        if part == 1:
            own_piola, own_plastic = piola, plastic_new
    for s in range(6):
        results[pl.ds((3 + s) * 8, 8), :] = own_plastic[s]
    lean = sums[1][15:18]
    force = [sum(own_piola[3 * a + b] * lean[b] for b in range(3)) for a in range(3)]

    for slot, (sy, sz, x_steps) in enumerate(OFFSETS):
        shift = -(8 * sy + sz) % 128
        for c in range(9):
            ring, inner = piolas[c, 0:8, :], piolas[c, 8:16, :]
            if shift:
                ring, inner = pltpu.roll(ring, shift, 1), pltpu.roll(inner, shift, 1)
            rolled_piolas[slot, pl.ds(c * 24, 8), :] = ring
            rolled_piolas[slot, pl.ds(c * 24 + 8, 8), :] = inner
            rolled_piolas[slot, pl.ds(c * 24 + 16, 8), :] = ring
        for sx in x_steps:
            if (sx, sy, sz) == (0, 0, 0):
                continue
            g = [weights[slot, (sx + 2) * 3 + a] for a in range(3)]
            for a in range(3):
                for b in range(3):
                    other = rolled_piolas[slot, pl.ds((3 * a + b) * 24 + 8 + sx, 8), :]
                    force[a] = force[a] + other * g[b]

    volume = piece(6, 1)
    for a in range(3):
        results[pl.ds(a * 8, 8), :] = volume * force[a]
    for c in range(9, 16):
        results[pl.ds(c * 8, 8), :] = zero

    for bx in range(2):
        rows = [results[pl.ds(bx * 4 + x, COMPS, stride=8), :] for x in range(4)]
        for by in range(2):
            block = bx * 2 + by
            turned = [pltpu.roll(rows[x], 32 * (x - by - 1) % 128, 1) for x in range(4)]
            low = jnp.where(chunk == 0, turned[0], turned[1])
            high = jnp.where(chunk == 2, turned[2], turned[3])
            value = exact_product(jnp.where(chunk < 2, low, high), onehots[block], 0)
            lanes = pl.ds(block * BLOCK, BLOCK)
            force_ref[:, lanes] = value[0:3]
            plastic_out_ref[:, lanes] = value[3:9]


def solution(mesh):
    n_gx, n_gy = mesh.shape["gx"], mesh.shape["gy"]

    def on_device(ref_pos, disp, volume, plastic, material, pair_list, pair_count):
        count = ref_pos.shape[1]
        vmem = pl.BlockSpec(memory_space=pltpu.VMEM)
        inputs = [
            pltpu.with_memory_space_constraint(array, pltpu.HBM)
            for array in (
                ref_pos, disp, volume.reshape(1, count), plastic, material.reshape(1, count)
            )
        ]
        region, onehots = pl.pallas_call(
            functools.partial(exchange_kernel, n_gx, n_gy),
            out_shape=(
                jax.ShapeDtypeStruct((4, 4, COMPS, BLOCK), F32),
                jax.ShapeDtypeStruct((4, BLOCK, BLOCK), jnp.bfloat16),
            ),
            in_specs=[pl.BlockSpec(memory_space=pltpu.HBM)] * 5,
            out_specs=(vmem, vmem),
            scratch_shapes=[
                pltpu.VMEM((3, count), F32),
                pltpu.VMEM((3, count), F32),
                pltpu.VMEM((1, count), F32),
                pltpu.VMEM((6, count), F32),
                pltpu.VMEM((1, count), jnp.int32),
                pltpu.VMEM((4, COMPS, BLOCK), F32),
                pltpu.SemaphoreType.DMA((5,)),
                pltpu.SemaphoreType.DMA((8,)),
                pltpu.SemaphoreType.DMA((8,)),
            ],
            compiler_params=pltpu.CompilerParams(
                collective_id=0, has_side_effects=True, vmem_limit_bytes=4 << 20
            ),
        )(*inputs)
        return pl.pallas_call(
            stencil_kernel,
            out_shape=(
                jax.ShapeDtypeStruct((3, count), F32),
                jax.ShapeDtypeStruct((6, count), F32),
            ),
            in_specs=[vmem] * 2,
            out_specs=(vmem, vmem),
            scratch_shapes=[
                pltpu.VMEM((COMPS * 16, BLOCK), F32),
                pltpu.VMEM((25, 7 * 32, BLOCK), F32),
                pltpu.VMEM((25, 15, 8, BLOCK), F32),
                pltpu.VMEM((9, 16, BLOCK), F32),
                pltpu.VMEM((25, 9 * 24, BLOCK), F32),
                pltpu.VMEM((COMPS * 8, BLOCK), F32),
            ],
            compiler_params=pltpu.CompilerParams(vmem_limit_bytes=16 << 20),
        )(region, onehots)

    in_specs = (
        P(None, ("gx", "gy")),
        P(None, ("gx", "gy")),
        P(("gx", "gy")),
        P(None, ("gx", "gy")),
        P(("gx", "gy")),
        P(("gx", "gy"), None, None),
        P(("gx", "gy")),
    )
    out_specs = (P(None, ("gx", "gy")), P(None, ("gx", "gy")))
    return jax.shard_map(
        on_device, mesh=mesh, in_specs=in_specs, out_specs=out_specs, check_vma=False
    )
```

```python
import functools

import jax
import jax.numpy as jnp
from jax import lax
from jax.experimental import pallas as pl
from jax.experimental.pallas import tpu as pltpu
from jax.sharding import PartitionSpec as P

BLOCK = 128
COMPS, VOLUME = 16, 14
RING_STEPS = (-2, -1, 0)
SHIFT = 0.1
SYM = ((0, 0), (1, 1), (2, 2), (0, 1), (0, 2), (1, 2))
DIRS = ((-1, -1), (-1, 1), (1, -1), (1, 1), (0, -1), (0, 1), (-1, 0), (1, 0))
MESH = pl.DeviceIdType.MESH


def within_reach(sx, sy, sz):
    return sum(max(abs(step) - 0.6, 0.0) ** 2 for step in (sx, sy, sz)) < 4.0


STEPS = range(-2, 3)
OFFSETS = tuple(
    (sy, sz, tuple(sx for sx in STEPS if within_reach(sx, sy, sz))) for sy in STEPS for sz in STEPS
)
F32 = jnp.float32


def exact_product(values, onehot, contract):
    high = values.astype(jnp.bfloat16)
    rest = values - high.astype(F32)
    mid = rest.astype(jnp.bfloat16)
    low = (rest - mid.astype(F32)).astype(jnp.bfloat16)
    parts = jnp.concatenate([high, mid, low], axis=0)
    out = lax.dot_general(parts, onehot, (((1,), (contract,)), ((), ())), preferred_element_type=F32)
    return out[0:16] + out[16:32] + out[32:48]


def send_range(step):
    if step == 0:
        return (1, 2), 1
    return ((2, 1), 0) if step == 1 else ((1, 1), 3)


def constitutive(moment, strain_sum, plastic, material):
    m00, m11, m22 = moment[0] + SHIFT, moment[1] + SHIFT, moment[2] + SHIFT
    m01, m02, m12 = moment[3:6]
    c00 = m11 * m22 - m12 * m12
    c01 = m02 * m12 - m01 * m22
    c02 = m01 * m12 - m02 * m11
    c11 = m00 * m22 - m02 * m02
    c12 = m01 * m02 - m00 * m12
    c22 = m00 * m11 - m01 * m01
    inverse = 1.0 / (m00 * c00 + m01 * c01 + m02 * c02)
    c00, c01, c02, c11, c12, c22 = [inverse * c for c in (c00, c01, c02, c11, c12, c22)]
    correct = [[c00, c01, c02], [c01, c11, c12], [c02, c12, c22]]
    grad = [
        [sum(strain_sum[3 * a + k] * correct[k][b] for k in range(3)) for b in range(3)]
        for a in range(3)
    ]
    strain = [0.5 * (grad[a][b] + grad[b][a]) - plastic[s] for s, (a, b) in enumerate(SYM)]
    first, second = material == 0.0, material == 1.0
    shear = jnp.where(first, 30.0, jnp.where(second, 40.0, 60.0))
    bulk = jnp.where(first, 60.0, jnp.where(second, 80.0, 120.0))
    yield_stress = jnp.where(first, 1.0, jnp.where(second, 1.4, 2.2))
    trace = strain[0] + strain[1] + strain[2]
    third = trace * (1.0 / 3.0)
    dev = [strain[s] - third if s < 3 else strain[s] for s in range(6)]
    trial = [2.0 * shear * value for value in dev]
    squares = (trial[0] ** 2 + trial[1] ** 2 + trial[2] ** 2) + 2.0 * (
        trial[3] ** 2 + trial[4] ** 2 + trial[5] ** 2
    )
    factor = yield_stress / jnp.maximum(jnp.sqrt(1.5 * squares), yield_stress)
    plastic_new = [plastic[s] + (1.0 - factor) * dev[s] for s in range(6)]
    pressure = bulk * trace
    s0, s1, s2, s3, s4, s5 = [
        factor * trial[s] + pressure if s < 3 else factor * trial[s] for s in range(6)
    ]
    full = [[s0, s3, s4], [s3, s1, s5], [s4, s5, s2]]
    piola = [
        full[a][0] * correct[0][b] + full[a][1] * correct[1][b] + full[a][2] * correct[2][b]
        for a in range(3)
        for b in range(3)
    ]
    return piola, plastic_new


def exchange_kernel(
    n_gx,
    n_gy,
    ref_hbm,
    disp_hbm,
    vol_hbm,
    plastic_hbm,
    material_hbm,
    region,
    onehots,
    ref_ref,
    disp_ref,
    vol_ref,
    plastic_ref,
    material_ref,
    packed,
    load_sem,
    send_sem,
    recv_sem,
):
    loads = [
        pltpu.make_async_copy(source, target, load_sem.at[number])
        for number, (source, target) in enumerate(
            (
                (ref_hbm, ref_ref),
                (disp_hbm, disp_ref),
                (vol_hbm, vol_ref),
                (plastic_hbm, plastic_ref),
                (material_hbm, material_ref),
            )
        )
    ]
    for load in loads:
        load.start()
    gx = lax.axis_index("gx")
    gy = lax.axis_index("gy")

    def present(dx, dy):
        conditions = []
        if dx:
            conditions.append(gx < n_gx - 1 if dx > 0 else gx > 0)
        if dy:
            conditions.append(gy < n_gy - 1 if dy > 0 else gy > 0)
        return functools.reduce(jnp.logical_and, conditions)

    fill_row = lax.broadcasted_iota(jnp.int32, (COMPS, BLOCK), 0)
    far = 4096.0 + 8.0 * lax.broadcasted_iota(jnp.int32, (COMPS, BLOCK), 1).astype(F32)
    for rx in range(4):
        for ry in range(4):
            if rx in (0, 3) or ry in (0, 3):
                region[rx, ry] = jnp.where(fill_row == 0, far + 4096.0 * (rx * 4 + ry), 0.0)

    barrier = pltpu.get_barrier_semaphore()
    for dx, dy in DIRS:

        @pl.when(present(dx, dy))
        def _():
            pl.semaphore_signal(
                barrier, inc=1, device_id={"gx": gx + dx, "gy": gy + dy}, device_id_type=MESH
            )

    for load in loads:
        load.wait()

    row_index = lax.broadcasted_iota(jnp.int32, (BLOCK, BLOCK), 0).astype(F32)
    for block in range(4):
        lanes = pl.ds(block * BLOCK, BLOCK)
        packed[block, 0:3, :] = ref_ref[:, lanes]
        packed[block, 3:6, :] = disp_ref[:, lanes]
        packed[block, 6:7, :] = vol_ref[:, lanes] * (1.5 / 8.0)
        packed[block, 7:13, :] = plastic_ref[:, lanes]
        packed[block, 13:14, :] = material_ref[:, lanes].astype(F32)
        packed[block, 14:15, :] = vol_ref[:, lanes]
        packed[block, 15:16, :] = jnp.zeros((1, BLOCK), F32)
        near = jnp.floor(ref_ref[:, lanes] + 0.5)
        near = near - jnp.min(near, axis=1, keepdims=True)
        site = near[0:1] * 32.0 + near[1:2] * 8.0 + near[2:3]
        onehot = jnp.where(row_index == site, 1.0, 0.0).astype(jnp.bfloat16)
        onehots[block] = onehot
        region[1 + block // 2, 1 + block % 2] = exact_product(packed[block], onehot, 1)

    beside = [
        1 + (place > 0).astype(jnp.int32) + (place < size - 1).astype(jnp.int32)
        for place, size in ((gx, n_gx), (gy, n_gy))
    ]
    pl.semaphore_wait(barrier, beside[0] * beside[1] - 1)

    def copy_to(number):
        dx, dy = DIRS[number]
        (sx, nx), tx = send_range(dx)
        (sy, ny), ty = send_range(dy)
        return pltpu.make_async_remote_copy(
            src_ref=region.at[pl.ds(sx, nx), pl.ds(sy, ny)],
            dst_ref=region.at[pl.ds(tx, nx), pl.ds(ty, ny)],
            send_sem=send_sem.at[number],
            recv_sem=recv_sem.at[number],
            device_id={"gx": gx + dx, "gy": gy + dy},
            device_id_type=MESH,
        )

    for number, (dx, dy) in enumerate(DIRS):

        @pl.when(present(dx, dy))
        def _():
            copy_to(number).start()

    for number, (dx, dy) in enumerate(DIRS):

        @pl.when(present(-dx, -dy))
        def _():
            copy_to(number).wait_recv()

    for number, (dx, dy) in enumerate(DIRS):

        @pl.when(present(dx, dy))
        def _():
            copy_to(number).wait_send()


def stencil_kernel(
    region,
    onehots,
    force_ref,
    plastic_out_ref,
    state,
    pairs,
    rolled,
    weights,
    piolas,
    rolled_piolas,
    results,
):
    chunk = lax.broadcasted_iota(jnp.int32, (COMPS, BLOCK), 1) // 32
    for rx in range(4):
        blocks = [region[rx, ry] for ry in range(4)]
        for x in range(4):
            turned = [
                pltpu.roll(blocks[ry], 32 * (ry - x) % 128, 1) if ry != x else blocks[ry]
                for ry in range(4)
            ]
            low = jnp.where(chunk == 0, turned[0], turned[1])
            high = jnp.where(chunk == 2, turned[2], turned[3])
            value = jnp.where(chunk < 2, low, high)
            row = (rx * 4 + x + 4) % 16
            state[pl.ds(row, COMPS, stride=24), :] = value
            if row < 8:
                state[pl.ds(row + 16, COMPS, stride=24), :] = value

    def rows(comp, start):
        return state[pl.ds(comp * 24 + start, 8), :]

    lower = lax.broadcasted_iota(jnp.int32, (8, BLOCK), 0) < 4

    def ring_rows(comp, step):
        return jnp.where(lower, rows(comp, 6 + step), rows(comp, 12 + step))

    twice = lax.broadcasted_iota(jnp.int32, (8, BLOCK), 0) % 4 < 2
    for step in RING_STEPS:
        for c in range(7):
            pairs[step + 2, c] = ring_rows(c, step)

    def doubled(value):
        return jnp.where(twice, value, pltpu.roll(value, 2, 0))

    z_lane = lax.broadcasted_iota(jnp.int32, (8, BLOCK), 1) % 8
    home = [[doubled(ring_rows(c, 0)) for c in range(3)], [rows(c, 8) for c in range(3)]]

    def add_visit(acc, place, other, reach, shift, alone=True):
        if shift:
            other = [pltpu.roll(value, shift, 1) for value in other]
        dX = [other[a] - place[a] for a in range(3)]
        square = dX[0] * dX[0] + dX[1] * dX[1] + dX[2] * dX[2]
        dist = square * lax.rsqrt(square if alone else jnp.maximum(square, 1e-20))
        t = jnp.maximum(reach - dist, 0.0)
        w = (other[6] * t) * (t * t)
        g = [w * dX[a] for a in range(3)]
        for s, (a, b) in enumerate(SYM):
            acc[s] = acc[s] + g[a] * dX[b]
        for a in range(3):
            for b in range(3):
                acc[6 + 3 * a + b] = acc[6 + 3 * a + b] + other[3 + a] * g[b]
        for a in range(3):
            acc[15 + a] = acc[15 + a] + g[a]
        return g

    def moment_visit(slot, sy, sz, x_steps, sums):
        shift = -(8 * sy + sz) % 128
        inside = (z_lane + sz >= 0) & (z_lane + sz < 8)
        reach = jnp.where(inside, 2.0, -100.0)
        for c in range(7):
            ring, inner = rows(c, 0), rows(c, 8)
            if shift:
                ring, inner = pltpu.roll(ring, shift, 1), pltpu.roll(inner, shift, 1)
            rolled[slot, pl.ds(c * 24, 8), :] = ring
            rolled[slot, pl.ds(c * 24 + 8, 8), :] = inner
            rolled[slot, pl.ds(c * 24 + 16, 8), :] = ring
        for sx in x_steps:
            if (sx, sy, sz) == (0, 0, 0):
                continue
            other = [rolled[slot, pl.ds(c * 24 + 8 + sx, 8), :] for c in range(7)]
            g = add_visit(sums[1], home[1], other, reach, 0)
            for a in range(3):
                weights[slot, (sx + 2) * 3 + a] = g[a]
        for step in RING_STEPS:
            if step == 0 and 2 not in x_steps or step == -1 and 1 not in x_steps:
                continue
            limit = reach if step < 0 else jnp.where(twice, -100.0, reach)
            add_visit(sums[0], home[0], [pairs[step + 2, c] for c in range(7)], limit, shift, shift != 0)

    zero = jnp.zeros((8, BLOCK), F32)
    sums = [[zero] * 18 for _ in range(2)]
    for slot, (sy, sz, x_steps) in enumerate(OFFSETS):
        moment_visit(slot, sy, sz, x_steps, sums)

    sums[0] = [value + pltpu.roll(value, 6, 0) for value in sums[0]]
    own_piola, own_plastic = None, None
    for part, acc in enumerate(sums):
        local = [rows(c, 8) if part == 1 else ring_rows(c, 0) for c in range(COMPS)]
        strain_sum = [acc[6 + 3 * a + b] - local[3 + a] * acc[15 + b] for a in range(3) for b in range(3)]
        piola, plastic_new = constitutive(acc[0:6], strain_sum, local[7:13], local[13])
        for c in range(9):
            if part == 1:
                piolas[c, 8:16, :] = piola[c]
            else:
                piolas[c, 6:8, :] = piola[c][0:2]
                piolas[c, 0:2, :] = piola[c][4:6]
        if part == 1:
            own_piola, own_plastic = piola, plastic_new
    for s in range(6):
        results[pl.ds((3 + s) * 8, 8), :] = own_plastic[s]
    lean = sums[1][15:18]
    force = [sum(own_piola[3 * a + b] * lean[b] for b in range(3)) for a in range(3)]

    for slot, (sy, sz, x_steps) in enumerate(OFFSETS):
        shift = -(8 * sy + sz) % 128
        for c in range(9):
            ring, inner = piolas[c, 0:8, :], piolas[c, 8:16, :]
            if shift:
                ring, inner = pltpu.roll(ring, shift, 1), pltpu.roll(inner, shift, 1)
            rolled_piolas[slot, pl.ds(c * 24, 8), :] = ring
            rolled_piolas[slot, pl.ds(c * 24 + 8, 8), :] = inner
            rolled_piolas[slot, pl.ds(c * 24 + 16, 8), :] = ring
        for sx in x_steps:
            if (sx, sy, sz) == (0, 0, 0):
                continue
            g = [weights[slot, (sx + 2) * 3 + a] for a in range(3)]
            for a in range(3):
                for b in range(3):
                    other = rolled_piolas[slot, pl.ds((3 * a + b) * 24 + 8 + sx, 8), :]
                    force[a] = force[a] + other * g[b]

    volume = rows(VOLUME, 8)
    for a in range(3):
        results[pl.ds(a * 8, 8), :] = volume * force[a]
    for c in range(9, 16):
        results[pl.ds(c * 8, 8), :] = zero

    for bx in range(2):
        lines = [results[pl.ds(bx * 4 + x, COMPS, stride=8), :] for x in range(4)]
        for by in range(2):
            block = bx * 2 + by
            turned = [pltpu.roll(lines[x], 32 * (x - by - 1) % 128, 1) for x in range(4)]
            low = jnp.where(chunk == 0, turned[0], turned[1])
            high = jnp.where(chunk == 2, turned[2], turned[3])
            value = exact_product(jnp.where(chunk < 2, low, high), onehots[block], 0)
            lanes = pl.ds(block * BLOCK, BLOCK)
            force_ref[:, lanes] = value[0:3]
            plastic_out_ref[:, lanes] = value[3:9]


def solution(mesh):
    n_gx, n_gy = mesh.shape["gx"], mesh.shape["gy"]

    def on_device(ref_pos, disp, volume, plastic, material, pair_list, pair_count):
        count = ref_pos.shape[1]
        vmem = pl.BlockSpec(memory_space=pltpu.VMEM)
        inputs = [
            pltpu.with_memory_space_constraint(array, pltpu.HBM)
            for array in (
                ref_pos, disp, volume.reshape(1, count), plastic, material.reshape(1, count)
            )
        ]
        region, onehots = pl.pallas_call(
            functools.partial(exchange_kernel, n_gx, n_gy),
            out_shape=(
                jax.ShapeDtypeStruct((4, 4, COMPS, BLOCK), F32),
                jax.ShapeDtypeStruct((4, BLOCK, BLOCK), jnp.bfloat16),
            ),
            in_specs=[pl.BlockSpec(memory_space=pltpu.HBM)] * 5,
            out_specs=(vmem, vmem),
            scratch_shapes=[
                pltpu.VMEM((3, count), F32),
                pltpu.VMEM((3, count), F32),
                pltpu.VMEM((1, count), F32),
                pltpu.VMEM((6, count), F32),
                pltpu.VMEM((1, count), jnp.int32),
                pltpu.VMEM((4, COMPS, BLOCK), F32),
                pltpu.SemaphoreType.DMA((5,)),
                pltpu.SemaphoreType.DMA((8,)),
                pltpu.SemaphoreType.DMA((8,)),
            ],
            compiler_params=pltpu.CompilerParams(
                collective_id=0, has_side_effects=True, vmem_limit_bytes=4 << 20
            ),
        )(*inputs)
        return pl.pallas_call(
            stencil_kernel,
            out_shape=(
                jax.ShapeDtypeStruct((3, count), F32),
                jax.ShapeDtypeStruct((6, count), F32),
            ),
            in_specs=[vmem] * 2,
            out_specs=(vmem, vmem),
            scratch_shapes=[
                pltpu.VMEM((COMPS * 24, BLOCK), F32),
                pltpu.VMEM((3, 7, 8, BLOCK), F32),
                pltpu.VMEM((25, 7 * 24, BLOCK), F32),
                pltpu.VMEM((25, 15, 8, BLOCK), F32),
                pltpu.VMEM((9, 16, BLOCK), F32),
                pltpu.VMEM((25, 9 * 24, BLOCK), F32),
                pltpu.VMEM((COMPS * 8, BLOCK), F32),
            ],
            compiler_params=pltpu.CompilerParams(vmem_limit_bytes=16 << 20),
        )(region, onehots)

    in_specs = (
        P(None, ("gx", "gy")),
        P(None, ("gx", "gy")),
        P(("gx", "gy")),
        P(None, ("gx", "gy")),
        P(("gx", "gy")),
        P(("gx", "gy"), None, None),
        P(("gx", "gy")),
    )
    out_specs = (P(None, ("gx", "gy")), P(None, ("gx", "gy")))
    return jax.shard_map(
        on_device, mesh=mesh, in_specs=in_specs, out_specs=out_specs, check_vma=False
    )
```

```python
import functools

import jax
import jax.numpy as jnp
from jax import lax
from jax.experimental import pallas as pl
from jax.experimental.pallas import tpu as pltpu
from jax.sharding import PartitionSpec as P

BLOCK = 128
COMPS, VOLUME = 16, 14
RING_STEPS = (-2, -1, 0)
BEYOND = {2: (0,), 3: (1, 2, 3), 12: (4, 5, 6), 13: (7,)}
SHIFT = 0.1
SYM = ((0, 0), (1, 1), (2, 2), (0, 1), (0, 2), (1, 2))
DIRS = ((0, -1), (0, 1), (-1, -1), (-1, 1), (1, -1), (1, 1), (-1, 0), (1, 0))
MESH = pl.DeviceIdType.MESH


def within_reach(sx, sy, sz):
    return sum(max(abs(step) - 0.6, 0.0) ** 2 for step in (sx, sy, sz)) < 4.0


STEPS = range(-2, 3)
OFFSETS = tuple(
    (sy, sz, tuple(sx for sx in STEPS if within_reach(sx, sy, sz))) for sy in STEPS for sz in STEPS
)
F32 = jnp.float32


def exact_product(values, onehot, contract):
    high = values.astype(jnp.bfloat16)
    rest = values - high.astype(F32)
    mid = rest.astype(jnp.bfloat16)
    low = (rest - mid.astype(F32)).astype(jnp.bfloat16)
    parts = jnp.concatenate([high, mid, low], axis=0)
    out = lax.dot_general(parts, onehot, (((1,), (contract,)), ((), ())), preferred_element_type=F32)
    return out[0:16] + out[16:32] + out[32:48]


def send_range(step):
    if step == 0:
        return (1, 2), 1
    return ((2, 1), 0) if step == 1 else ((1, 1), 3)


def constitutive(moment, strain_sum, plastic, material):
    m00, m11, m22 = moment[0] + SHIFT, moment[1] + SHIFT, moment[2] + SHIFT
    m01, m02, m12 = moment[3:6]
    c00 = m11 * m22 - m12 * m12
    c01 = m02 * m12 - m01 * m22
    c02 = m01 * m12 - m02 * m11
    c11 = m00 * m22 - m02 * m02
    c12 = m01 * m02 - m00 * m12
    c22 = m00 * m11 - m01 * m01
    inverse = 1.0 / (m00 * c00 + m01 * c01 + m02 * c02)
    c00, c01, c02, c11, c12, c22 = [inverse * c for c in (c00, c01, c02, c11, c12, c22)]
    correct = [[c00, c01, c02], [c01, c11, c12], [c02, c12, c22]]
    grad = [
        [sum(strain_sum[3 * a + k] * correct[k][b] for k in range(3)) for b in range(3)]
        for a in range(3)
    ]
    strain = [0.5 * (grad[a][b] + grad[b][a]) - plastic[s] for s, (a, b) in enumerate(SYM)]
    first, second = material == 0.0, material == 1.0
    shear = jnp.where(first, 30.0, jnp.where(second, 40.0, 60.0))
    bulk = jnp.where(first, 60.0, jnp.where(second, 80.0, 120.0))
    yield_stress = jnp.where(first, 1.0, jnp.where(second, 1.4, 2.2))
    trace = strain[0] + strain[1] + strain[2]
    third = trace * (1.0 / 3.0)
    dev = [strain[s] - third if s < 3 else strain[s] for s in range(6)]
    trial = [2.0 * shear * value for value in dev]
    squares = (trial[0] ** 2 + trial[1] ** 2 + trial[2] ** 2) + 2.0 * (
        trial[3] ** 2 + trial[4] ** 2 + trial[5] ** 2
    )
    factor = yield_stress / jnp.maximum(jnp.sqrt(1.5 * squares), yield_stress)
    plastic_new = [plastic[s] + (1.0 - factor) * dev[s] for s in range(6)]
    pressure = bulk * trace
    s0, s1, s2, s3, s4, s5 = [
        factor * trial[s] + pressure if s < 3 else factor * trial[s] for s in range(6)
    ]
    full = [[s0, s3, s4], [s3, s1, s5], [s4, s5, s2]]
    piola = [
        full[a][0] * correct[0][b] + full[a][1] * correct[1][b] + full[a][2] * correct[2][b]
        for a in range(3)
        for b in range(3)
    ]
    return piola, plastic_new


def reach_of(sz):
    z_lane = lax.broadcasted_iota(jnp.int32, (8, BLOCK), 1) % 8
    return jnp.where((z_lane + sz >= 0) & (z_lane + sz < 8), 2.0, -100.0)


def lane_turn(sy, sz):
    return -(8 * sy + sz) % 128


def turn(values, shift):
    return [pltpu.roll(value, shift, 1) for value in values] if shift else list(values)


def rows_of_blocks(blocks, x):
    chunk = lax.broadcasted_iota(jnp.int32, (COMPS, BLOCK), 1) // 32
    turned = [
        pltpu.roll(blocks[ry], 32 * (ry - x) % 128, 1) if ry != x else blocks[ry] for ry in range(4)
    ]
    low = jnp.where(chunk == 0, turned[0], turned[1])
    high = jnp.where(chunk == 2, turned[2], turned[3])
    return jnp.where(chunk < 2, low, high)


def add_visit(acc, place, other, reach, alone):
    dX = [other[a] - place[a] for a in range(3)]
    square = dX[0] * dX[0] + dX[1] * dX[1] + dX[2] * dX[2]
    dist = square * lax.rsqrt(square if alone else jnp.maximum(square, 1e-20))
    t = jnp.maximum(reach - dist, 0.0)
    w = (other[6] * t) * (t * t)
    g = [w * dX[a] for a in range(3)]
    for s, (a, b) in enumerate(SYM):
        acc[s] = acc[s] + g[a] * dX[b]
    for a in range(3):
        for b in range(3):
            acc[6 + 3 * a + b] = acc[6 + 3 * a + b] + other[3 + a] * g[b]
    for a in range(3):
        acc[15 + a] = acc[15 + a] + g[a]
    return g


def exchange_kernel(
    n_gx,
    n_gy,
    ref_hbm,
    disp_hbm,
    vol_hbm,
    plastic_hbm,
    material_hbm,
    region,
    onehots,
    core,
    core_sums,
    weights,
    ref_ref,
    disp_ref,
    vol_ref,
    plastic_ref,
    material_ref,
    packed,
    rolled,
    load_sem,
    send_sem,
    recv_sem,
):
    loads = [
        pltpu.make_async_copy(source, target, load_sem.at[number])
        for number, (source, target) in enumerate(
            (
                (ref_hbm, ref_ref),
                (disp_hbm, disp_ref),
                (vol_hbm, vol_ref),
                (plastic_hbm, plastic_ref),
                (material_hbm, material_ref),
            )
        )
    ]
    for load in loads:
        load.start()
    gx = lax.axis_index("gx")
    gy = lax.axis_index("gy")

    def present(dx, dy):
        conditions = []
        if dx:
            conditions.append(gx < n_gx - 1 if dx > 0 else gx > 0)
        if dy:
            conditions.append(gy < n_gy - 1 if dy > 0 else gy > 0)
        return functools.reduce(jnp.logical_and, conditions)

    fill_row = lax.broadcasted_iota(jnp.int32, (COMPS, BLOCK), 0)
    far = 4096.0 + 8.0 * lax.broadcasted_iota(jnp.int32, (COMPS, BLOCK), 1).astype(F32)
    for rx in range(4):
        for ry in range(4):
            if rx in (0, 3) or ry in (0, 3):
                region[rx, ry] = jnp.where(fill_row == 0, far + 4096.0 * (rx * 4 + ry), 0.0)

    barrier = pltpu.get_barrier_semaphore()
    for dx, dy in DIRS:

        @pl.when(present(dx, dy))
        def _():
            pl.semaphore_signal(
                barrier, inc=1, device_id={"gx": gx + dx, "gy": gy + dy}, device_id_type=MESH
            )

    for load in loads:
        load.wait()

    row_index = lax.broadcasted_iota(jnp.int32, (BLOCK, BLOCK), 0).astype(F32)
    for block in range(4):
        lanes = pl.ds(block * BLOCK, BLOCK)
        packed[block, 0:3, :] = ref_ref[:, lanes]
        packed[block, 3:6, :] = disp_ref[:, lanes]
        packed[block, 6:7, :] = vol_ref[:, lanes] * (1.5 / 8.0)
        packed[block, 7:13, :] = plastic_ref[:, lanes]
        packed[block, 13:14, :] = material_ref[:, lanes].astype(F32)
        packed[block, 14:15, :] = vol_ref[:, lanes]
        packed[block, 15:16, :] = jnp.zeros((1, BLOCK), F32)
        near = jnp.floor(ref_ref[:, lanes] + 0.5)
        near = near - jnp.min(near, axis=1, keepdims=True)
        site = near[0:1] * 32.0 + near[1:2] * 8.0 + near[2:3]
        onehot = jnp.where(row_index == site, 1.0, 0.0).astype(jnp.bfloat16)
        onehots[block] = onehot
        region[1 + block // 2, 1 + block % 2] = exact_product(packed[block], onehot, 1)

    beside = [
        1 + (place > 0).astype(jnp.int32) + (place < size - 1).astype(jnp.int32)
        for place, size in ((gx, n_gx), (gy, n_gy))
    ]
    pl.semaphore_wait(barrier, beside[0] * beside[1] - 1)

    def copy_to(number):
        dx, dy = DIRS[number]
        (sx, nx), tx = send_range(dx)
        (sy, ny), ty = send_range(dy)
        return pltpu.make_async_remote_copy(
            src_ref=region.at[pl.ds(sx, nx), pl.ds(sy, ny)],
            dst_ref=region.at[pl.ds(tx, nx), pl.ds(ty, ny)],
            send_sem=send_sem.at[number],
            recv_sem=recv_sem.at[number],
            device_id={"gx": gx + dx, "gy": gy + dy},
            device_id_type=MESH,
        )

    for number, (dx, dy) in enumerate(DIRS):

        @pl.when(present(dx, dy))
        def _():
            copy_to(number).start()

    def receive(chosen):
        for number, (dx, dy) in enumerate(DIRS):
            if chosen(dx):
                pl.when(present(-dx, -dy))(lambda number=number: copy_to(number).wait_recv())

    receive(lambda dx: dx == 0)
    for rx in (1, 2):
        blocks = [region[rx, ry] for ry in range(4)]
        for x in range(4):
            core[pl.ds(rx * 4 + x - 4, COMPS, stride=8), :] = rows_of_blocks(blocks, x)
    row = lax.broadcasted_iota(jnp.int32, (8, BLOCK), 0)
    zero = jnp.zeros((8, BLOCK), F32)
    home = [core[pl.ds(c * 8, 8), :] for c in range(7)]
    sums = [zero] * 18
    for slot, (sy, sz, x_steps) in enumerate(OFFSETS):
        rolled[slot, 0:8, :] = zero
        rolled[slot, 64:72, :] = zero
        for c, value in enumerate(turn(home, lane_turn(sy, sz))):
            rolled[slot, pl.ds(8 + c * 8, 8), :] = value
        reach = reach_of(sz)
        for sx in x_steps:
            if (sx, sy, sz) == (0, 0, 0):
                continue
            other = [rolled[slot, pl.ds(8 + c * 8 + sx, 8), :] for c in range(7)]
            limit = jnp.where((row + sx >= 0) & (row + sx < 8), reach, -100.0) if sx else reach
            g = add_visit(sums, home, other, limit, sx == 0)
            for a in range(3):
                weights[slot, (sx + 2) * 3 + a] = g[a]
    for s in range(18):
        core_sums[s] = sums[s]

    receive(lambda dx: dx != 0)
    for number, (dx, dy) in enumerate(DIRS):

        @pl.when(present(dx, dy))
        def _():
            copy_to(number).wait_send()


def stencil_kernel(
    region,
    onehots,
    core,
    core_sums,
    weights,
    force_ref,
    plastic_out_ref,
    state,
    pairs,
    beyond,
    beyond_weights,
    rolled_piolas,
    results,
):
    for c in range(COMPS):
        state[pl.ds(c * 24 + 8, 8), :] = core[pl.ds(c * 8, 8), :]
    for rx in (0, 3):
        blocks = [region[rx, ry] for ry in range(4)]
        for x in range(4):
            value = rows_of_blocks(blocks, x)
            place = (rx * 4 + x + 4) % 16
            state[pl.ds(place, COMPS, stride=24), :] = value
            state[pl.ds(place + 16, COMPS, stride=24), :] = value
            for target in BEYOND.get(rx * 4 + x, ()):
                beyond[pl.ds(target, COMPS, stride=8), :] = value

    def rows(comp, start):
        return state[pl.ds(comp * 24 + start, 8), :]

    lower = lax.broadcasted_iota(jnp.int32, (8, BLOCK), 0) < 4

    def ring_rows(comp, step):
        return jnp.where(lower, rows(comp, 6 + step), rows(comp, 12 + step))

    twice = lax.broadcasted_iota(jnp.int32, (8, BLOCK), 0) % 4 < 2
    for step in RING_STEPS:
        for c in range(7):
            pairs[step + 2, c] = ring_rows(c, step)

    def doubled(value):
        return jnp.where(twice, value, pltpu.roll(value, 2, 0))

    row = lax.broadcasted_iota(jnp.int32, (8, BLOCK), 0)
    used = (row < 3) | (row > 4)

    def facing(value):
        return jnp.where(row == 2, pltpu.roll(value, 2, 0), jnp.where(row == 5, pltpu.roll(value, 6, 0), value))

    def gathered(value):
        paired = jnp.where(row == 0, pltpu.roll(value, 6, 0), jnp.where(row == 7, pltpu.roll(value, 2, 0), 0.0))
        return jnp.where((row < 2) | (row > 5), value + paired, 0.0)

    home = [doubled(ring_rows(c, 0)) for c in range(3)]
    edge = [facing(rows(c, 8)) for c in range(3)]
    sources = [beyond[pl.ds(c * 8, 8), :] for c in range(7)]
    zero = jnp.zeros((8, BLOCK), F32)
    ring_sums, edge_sums = [zero] * 18, [zero] * 18
    for slot, (sy, sz, x_steps) in enumerate(OFFSETS):
        shift = lane_turn(sy, sz)
        reach = reach_of(sz)
        for step in RING_STEPS:
            if step == 0 and 2 not in x_steps or step == -1 and 1 not in x_steps:
                continue
            limit = reach if step < 0 else jnp.where(twice, -100.0, reach)
            other = turn([pairs[step + 2, c] for c in range(7)], shift)
            add_visit(ring_sums, home, other, limit, shift != 0)
        if 1 in x_steps:
            limit = jnp.where(used, reach, -100.0)
            g = add_visit(edge_sums, edge, turn(sources, shift), limit, True)
            for a in range(3):
                beyond_weights[slot, a] = g[a]

    ring_sums = [value + pltpu.roll(value, 6, 0) for value in ring_sums]
    own_sums = [core_sums[s] + gathered(edge_sums[s]) for s in range(18)]

    def stresses(acc, local):
        strain_sum = [acc[6 + 3 * a + b] - local[3 + a] * acc[15 + b] for a in range(3) for b in range(3)]
        return constitutive(acc[0:6], strain_sum, local[7:13], local[13])

    own_piola, own_plastic = stresses(own_sums, [rows(c, 8) for c in range(COMPS)])
    ring_piola, _ = stresses(ring_sums, [ring_rows(c, 0) for c in range(COMPS)])
    ring_piola = [
        jnp.where(row < 2, value, jnp.where(row < 6, pltpu.roll(value, 1, 0), pltpu.roll(value, 2, 0)))
        for value in ring_piola
    ]
    for s in range(6):
        results[pl.ds((3 + s) * 8, 8), :] = own_plastic[s]
    lean = own_sums[15:18]
    force = [sum(own_piola[3 * a + b] * lean[b] for b in range(3)) for a in range(3)]
    edge_force = [zero] * 3
    for slot, (sy, sz, x_steps) in enumerate(OFFSETS):
        shift = lane_turn(sy, sz)
        rolled_piolas[slot, 0:8, :] = zero
        rolled_piolas[slot, 80:88, :] = zero
        for c, value in enumerate(turn(own_piola, shift)):
            rolled_piolas[slot, pl.ds(8 + c * 8, 8), :] = value
        for sx in x_steps:
            if (sx, sy, sz) == (0, 0, 0):
                continue
            g = [weights[slot, (sx + 2) * 3 + a] for a in range(3)]
            for a in range(3):
                for b in range(3):
                    other = rolled_piolas[slot, pl.ds(8 + (3 * a + b) * 8 + sx, 8), :]
                    force[a] = force[a] + other * g[b]
        if 1 in x_steps:
            other = turn(ring_piola, shift)
            for a in range(3):
                for b in range(3):
                    edge_force[a] = edge_force[a] + other[3 * a + b] * beyond_weights[slot, b]
    force = [force[a] + gathered(edge_force[a]) for a in range(3)]

    volume = rows(VOLUME, 8)
    for a in range(3):
        results[pl.ds(a * 8, 8), :] = volume * force[a]
    for c in range(9, 16):
        results[pl.ds(c * 8, 8), :] = zero

    chunk = lax.broadcasted_iota(jnp.int32, (COMPS, BLOCK), 1) // 32
    for bx in range(2):
        lines = [results[pl.ds(bx * 4 + x, COMPS, stride=8), :] for x in range(4)]
        for by in range(2):
            block = bx * 2 + by
            turned = [pltpu.roll(lines[x], 32 * (x - by - 1) % 128, 1) for x in range(4)]
            low = jnp.where(chunk == 0, turned[0], turned[1])
            high = jnp.where(chunk == 2, turned[2], turned[3])
            value = exact_product(jnp.where(chunk < 2, low, high), onehots[block], 0)
            lanes = pl.ds(block * BLOCK, BLOCK)
            force_ref[:, lanes] = value[0:3]
            plastic_out_ref[:, lanes] = value[3:9]


def solution(mesh):
    n_gx, n_gy = mesh.shape["gx"], mesh.shape["gy"]

    def on_device(ref_pos, disp, volume, plastic, material, pair_list, pair_count):
        count = ref_pos.shape[1]
        vmem = pl.BlockSpec(memory_space=pltpu.VMEM)
        inputs = [
            pltpu.with_memory_space_constraint(array, pltpu.HBM)
            for array in (
                ref_pos, disp, volume.reshape(1, count), plastic, material.reshape(1, count)
            )
        ]
        shared = pl.pallas_call(
            functools.partial(exchange_kernel, n_gx, n_gy),
            out_shape=(
                jax.ShapeDtypeStruct((4, 4, COMPS, BLOCK), F32),
                jax.ShapeDtypeStruct((4, BLOCK, BLOCK), jnp.bfloat16),
                jax.ShapeDtypeStruct((COMPS * 8, BLOCK), F32),
                jax.ShapeDtypeStruct((18, 8, BLOCK), F32),
                jax.ShapeDtypeStruct((25, 15, 8, BLOCK), F32),
            ),
            in_specs=[pl.BlockSpec(memory_space=pltpu.HBM)] * 5,
            out_specs=(vmem,) * 5,
            scratch_shapes=[
                pltpu.VMEM((3, count), F32),
                pltpu.VMEM((3, count), F32),
                pltpu.VMEM((1, count), F32),
                pltpu.VMEM((6, count), F32),
                pltpu.VMEM((1, count), jnp.int32),
                pltpu.VMEM((4, COMPS, BLOCK), F32),
                pltpu.VMEM((25, 72, BLOCK), F32),
                pltpu.SemaphoreType.DMA((5,)),
                pltpu.SemaphoreType.DMA((8,)),
                pltpu.SemaphoreType.DMA((8,)),
            ],
            compiler_params=pltpu.CompilerParams(
                collective_id=0, has_side_effects=True, vmem_limit_bytes=8 << 20
            ),
        )(*inputs)
        return pl.pallas_call(
            stencil_kernel,
            out_shape=(
                jax.ShapeDtypeStruct((3, count), F32),
                jax.ShapeDtypeStruct((6, count), F32),
            ),
            in_specs=[vmem] * 5,
            out_specs=(vmem, vmem),
            scratch_shapes=[
                pltpu.VMEM((COMPS * 24, BLOCK), F32),
                pltpu.VMEM((3, 7, 8, BLOCK), F32),
                pltpu.VMEM((COMPS * 8, BLOCK), F32),
                pltpu.VMEM((25, 3, 8, BLOCK), F32),
                pltpu.VMEM((25, 88, BLOCK), F32),
                pltpu.VMEM((COMPS * 8, BLOCK), F32),
            ],
            compiler_params=pltpu.CompilerParams(vmem_limit_bytes=16 << 20),
        )(*shared)

    in_specs = (
        P(None, ("gx", "gy")),
        P(None, ("gx", "gy")),
        P(("gx", "gy")),
        P(None, ("gx", "gy")),
        P(("gx", "gy")),
        P(("gx", "gy"), None, None),
        P(("gx", "gy")),
    )
    out_specs = (P(None, ("gx", "gy")), P(None, ("gx", "gy")))
    return jax.shard_map(
        on_device, mesh=mesh, in_specs=in_specs, out_specs=out_specs, check_vma=False
    )
```

```python
import functools

import jax
import jax.numpy as jnp
from jax import lax
from jax.experimental import pallas as pl
from jax.experimental.pallas import tpu as pltpu
from jax.sharding import PartitionSpec as P

BLOCK = 128
COMPS, VOLUME = 16, 14
RING_STEPS = (-2, -1, 0)
BEYOND = {2: (0,), 3: (1, 2, 3), 12: (4, 5, 6), 13: (7,)}
SHIFT = 0.1
SYM = ((0, 0), (1, 1), (2, 2), (0, 1), (0, 2), (1, 2))
DIRS = ((0, -1), (0, 1), (-1, -1), (-1, 1), (-1, 0), (1, -1), (1, 1), (1, 0))
MESH = pl.DeviceIdType.MESH


def within_reach(sx, sy, sz):
    return sum(max(abs(step) - 0.6, 0.0) ** 2 for step in (sx, sy, sz)) < 4.0


STEPS = range(-2, 3)
OFFSETS = tuple(
    (sy, sz, tuple(sx for sx in STEPS if within_reach(sx, sy, sz))) for sy in STEPS for sz in STEPS
)
F32 = jnp.float32


def exact_product(values, onehot, contract):
    high = values.astype(jnp.bfloat16)
    rest = values - high.astype(F32)
    mid = rest.astype(jnp.bfloat16)
    low = (rest - mid.astype(F32)).astype(jnp.bfloat16)
    parts = jnp.concatenate([high, mid, low], axis=0)
    out = lax.dot_general(parts, onehot, (((1,), (contract,)), ((), ())), preferred_element_type=F32)
    return out[0:16] + out[16:32] + out[32:48]


def send_range(step):
    if step == 0:
        return (1, 2), 1
    return ((2, 1), 0) if step == 1 else ((1, 1), 3)


def constitutive(moment, strain_sum, plastic, material):
    m00, m11, m22 = moment[0] + SHIFT, moment[1] + SHIFT, moment[2] + SHIFT
    m01, m02, m12 = moment[3:6]
    c00 = m11 * m22 - m12 * m12
    c01 = m02 * m12 - m01 * m22
    c02 = m01 * m12 - m02 * m11
    c11 = m00 * m22 - m02 * m02
    c12 = m01 * m02 - m00 * m12
    c22 = m00 * m11 - m01 * m01
    inverse = 1.0 / (m00 * c00 + m01 * c01 + m02 * c02)
    c00, c01, c02, c11, c12, c22 = [inverse * c for c in (c00, c01, c02, c11, c12, c22)]
    correct = [[c00, c01, c02], [c01, c11, c12], [c02, c12, c22]]
    grad = [
        [sum(strain_sum[3 * a + k] * correct[k][b] for k in range(3)) for b in range(3)]
        for a in range(3)
    ]
    strain = [0.5 * (grad[a][b] + grad[b][a]) - plastic[s] for s, (a, b) in enumerate(SYM)]
    first, second = material == 0.0, material == 1.0
    shear = jnp.where(first, 30.0, jnp.where(second, 40.0, 60.0))
    bulk = jnp.where(first, 60.0, jnp.where(second, 80.0, 120.0))
    yield_stress = jnp.where(first, 1.0, jnp.where(second, 1.4, 2.2))
    trace = strain[0] + strain[1] + strain[2]
    third = trace * (1.0 / 3.0)
    dev = [strain[s] - third if s < 3 else strain[s] for s in range(6)]
    trial = [2.0 * shear * value for value in dev]
    squares = (trial[0] ** 2 + trial[1] ** 2 + trial[2] ** 2) + 2.0 * (
        trial[3] ** 2 + trial[4] ** 2 + trial[5] ** 2
    )
    factor = yield_stress / jnp.maximum(jnp.sqrt(1.5 * squares), yield_stress)
    plastic_new = [plastic[s] + (1.0 - factor) * dev[s] for s in range(6)]
    pressure = bulk * trace
    s0, s1, s2, s3, s4, s5 = [
        factor * trial[s] + pressure if s < 3 else factor * trial[s] for s in range(6)
    ]
    full = [[s0, s3, s4], [s3, s1, s5], [s4, s5, s2]]
    piola = [
        full[a][0] * correct[0][b] + full[a][1] * correct[1][b] + full[a][2] * correct[2][b]
        for a in range(3)
        for b in range(3)
    ]
    return piola, plastic_new


def reach_of(sz):
    z_lane = lax.broadcasted_iota(jnp.int32, (8, BLOCK), 1) % 8
    return jnp.where((z_lane + sz >= 0) & (z_lane + sz < 8), 2.0, -100.0)


def lane_turn(sy, sz):
    return -(8 * sy + sz) % 128


def turn(values, shift):
    return [pltpu.roll(value, shift, 1) for value in values] if shift else list(values)


def rows_of_blocks(blocks, x):
    chunk = lax.broadcasted_iota(jnp.int32, (COMPS, BLOCK), 1) // 32
    turned = [
        pltpu.roll(blocks[ry], 32 * (ry - x) % 128, 1) if ry != x else blocks[ry] for ry in range(4)
    ]
    low = jnp.where(chunk == 0, turned[0], turned[1])
    high = jnp.where(chunk == 2, turned[2], turned[3])
    return jnp.where(chunk < 2, low, high)


def add_visit(acc, place, other, reach, alone):
    dX = [other[a] - place[a] for a in range(3)]
    square = dX[0] * dX[0] + dX[1] * dX[1] + dX[2] * dX[2]
    dist = square * lax.rsqrt(square if alone else jnp.maximum(square, 1e-20))
    t = jnp.maximum(reach - dist, 0.0)
    w = (other[6] * t) * (t * t)
    g = [w * dX[a] for a in range(3)]
    for s, (a, b) in enumerate(SYM):
        acc[s] = acc[s] + g[a] * dX[b]
    for a in range(3):
        for b in range(3):
            acc[6 + 3 * a + b] = acc[6 + 3 * a + b] + other[3 + a] * g[b]
    for a in range(3):
        acc[15 + a] = acc[15 + a] + g[a]
    return g


def exchange_kernel(
    n_gx,
    n_gy,
    ref_hbm,
    disp_hbm,
    vol_hbm,
    plastic_hbm,
    material_hbm,
    region,
    onehots,
    core,
    core_sums,
    weights,
    ref_ref,
    disp_ref,
    vol_ref,
    plastic_ref,
    material_ref,
    packed,
    inner,
    rolled,
    load_sem,
    send_sem,
    recv_sem,
):
    loads = [
        pltpu.make_async_copy(source, target, load_sem.at[number])
        for number, (source, target) in enumerate(
            (
                (ref_hbm, ref_ref),
                (disp_hbm, disp_ref),
                (vol_hbm, vol_ref),
                (plastic_hbm, plastic_ref),
                (material_hbm, material_ref),
            )
        )
    ]
    for load in loads:
        load.start()
    gx = lax.axis_index("gx")
    gy = lax.axis_index("gy")

    def present(dx, dy):
        conditions = []
        if dx:
            conditions.append(gx < n_gx - 1 if dx > 0 else gx > 0)
        if dy:
            conditions.append(gy < n_gy - 1 if dy > 0 else gy > 0)
        return functools.reduce(jnp.logical_and, conditions)

    fill_row = lax.broadcasted_iota(jnp.int32, (COMPS, BLOCK), 0)
    far = 4096.0 + 8.0 * lax.broadcasted_iota(jnp.int32, (COMPS, BLOCK), 1).astype(F32)
    for rx in range(4):
        for ry in range(4):
            if rx in (0, 3) or ry in (0, 3):
                region[rx, ry] = jnp.where(fill_row == 0, far + 4096.0 * (rx * 4 + ry), 0.0)

    barrier = pltpu.get_barrier_semaphore()
    for dx, dy in DIRS:

        @pl.when(present(dx, dy))
        def _():
            pl.semaphore_signal(
                barrier, inc=1, device_id={"gx": gx + dx, "gy": gy + dy}, device_id_type=MESH
            )

    for load in loads:
        load.wait()

    row_index = lax.broadcasted_iota(jnp.int32, (BLOCK, BLOCK), 0).astype(F32)
    for block in range(4):
        lanes = pl.ds(block * BLOCK, BLOCK)
        packed[block, 0:3, :] = ref_ref[:, lanes]
        packed[block, 3:6, :] = disp_ref[:, lanes]
        packed[block, 6:7, :] = vol_ref[:, lanes] * (1.5 / 8.0)
        packed[block, 7:13, :] = plastic_ref[:, lanes]
        packed[block, 13:14, :] = material_ref[:, lanes].astype(F32)
        packed[block, 14:15, :] = vol_ref[:, lanes]
        packed[block, 15:16, :] = jnp.zeros((1, BLOCK), F32)
        near = jnp.floor(ref_ref[:, lanes] + 0.5)
        near = near - jnp.min(near, axis=1, keepdims=True)
        site = near[0:1] * 32.0 + near[1:2] * 8.0 + near[2:3]
        onehot = jnp.where(row_index == site, 1.0, 0.0).astype(jnp.bfloat16)
        onehots[block] = onehot
        region[1 + block // 2, 1 + block % 2] = exact_product(packed[block], onehot, 1)

    beside = [
        1 + (place > 0).astype(jnp.int32) + (place < size - 1).astype(jnp.int32)
        for place, size in ((gx, n_gx), (gy, n_gy))
    ]
    pl.semaphore_wait(barrier, beside[0] * beside[1] - 1)

    def copy_to(number):
        dx, dy = DIRS[number]
        (sx, nx), tx = send_range(dx)
        (sy, ny), ty = send_range(dy)
        return pltpu.make_async_remote_copy(
            src_ref=region.at[pl.ds(sx, nx), pl.ds(sy, ny)],
            dst_ref=region.at[pl.ds(tx, nx), pl.ds(ty, ny)],
            send_sem=send_sem.at[number],
            recv_sem=recv_sem.at[number],
            device_id={"gx": gx + dx, "gy": gy + dy},
            device_id_type=MESH,
        )

    for number, (dx, dy) in enumerate(DIRS):

        @pl.when(present(dx, dy))
        def _():
            copy_to(number).start()

    def receive(chosen):
        for number, (dx, dy) in enumerate(DIRS):
            if chosen(dx):
                pl.when(present(-dx, -dy))(lambda number=number: copy_to(number).wait_recv())

    zero = jnp.zeros((8, BLOCK), F32)
    for slot in range(len(OFFSETS)):
        rolled[slot, 0:8, :] = zero
        rolled[slot, 64:72, :] = zero
    chunk = lax.broadcasted_iota(jnp.int32, (COMPS, BLOCK), 1) // 32
    for rx in (1, 2):
        blocks = [region[rx, 1], region[rx, 2]]
        for x in range(4):
            first, second = (pltpu.roll(blocks[k], 32 * (k + 1 - x) % 128, 1) for k in range(2))
            inner[rx * 4 + x - 4] = jnp.where(chunk == 1, first, second)
    receive(lambda dx: dx == 0)
    for rx in (1, 2):
        blocks = [region[rx, 0], region[rx, 3]]
        for x in range(4):
            first, last = (pltpu.roll(blocks[k], 32 * (3 * k - x) % 128, 1) for k in range(2))
            value = jnp.where(chunk == 0, first, jnp.where(chunk == 3, last, inner[rx * 4 + x - 4]))
            core[pl.ds(rx * 4 + x - 4, COMPS, stride=8), :] = value
    row = lax.broadcasted_iota(jnp.int32, (8, BLOCK), 0)
    home = [core[pl.ds(c * 8, 8), :] for c in range(7)]
    sums = [zero] * 18
    for slot, (sy, sz, x_steps) in enumerate(OFFSETS):
        for c, value in enumerate(turn(home, lane_turn(sy, sz))):
            rolled[slot, pl.ds(8 + c * 8, 8), :] = value
        reach = reach_of(sz)
        for sx in x_steps:
            if (sx, sy, sz) == (0, 0, 0):
                continue
            other = [rolled[slot, pl.ds(8 + c * 8 + sx, 8), :] for c in range(7)]
            limit = jnp.where((row + sx >= 0) & (row + sx < 8), reach, -100.0) if sx else reach
            g = add_visit(sums, home, other, limit, sx == 0)
            for a in range(3):
                weights[slot, (sx + 2) * 3 + a] = g[a]
    for s in range(18):
        core_sums[s] = sums[s]

    receive(lambda dx: dx != 0)
    for number, (dx, dy) in enumerate(DIRS):

        @pl.when(present(dx, dy))
        def _():
            copy_to(number).wait_send()


def stencil_kernel(
    region,
    onehots,
    core,
    core_sums,
    weights,
    force_ref,
    plastic_out_ref,
    state,
    pairs,
    beyond,
    beyond_weights,
    rolled_piolas,
    results,
):
    for c in range(COMPS):
        state[pl.ds(c * 24 + 8, 8), :] = core[pl.ds(c * 8, 8), :]
    for rx in (0, 3):
        blocks = [region[rx, ry] for ry in range(4)]
        for x in range(4):
            value = rows_of_blocks(blocks, x)
            place = (rx * 4 + x + 4) % 16
            state[pl.ds(place, COMPS, stride=24), :] = value
            state[pl.ds(place + 16, COMPS, stride=24), :] = value
            for target in BEYOND.get(rx * 4 + x, ()):
                beyond[pl.ds(target, COMPS, stride=8), :] = value

    def rows(comp, start):
        return state[pl.ds(comp * 24 + start, 8), :]

    lower = lax.broadcasted_iota(jnp.int32, (8, BLOCK), 0) < 4

    def ring_rows(comp, step):
        return jnp.where(lower, rows(comp, 6 + step), rows(comp, 12 + step))

    twice = lax.broadcasted_iota(jnp.int32, (8, BLOCK), 0) % 4 < 2
    for step in RING_STEPS:
        for c in range(7):
            pairs[step + 2, c] = ring_rows(c, step)

    def doubled(value):
        return jnp.where(twice, value, pltpu.roll(value, 2, 0))

    row = lax.broadcasted_iota(jnp.int32, (8, BLOCK), 0)
    used = (row < 3) | (row > 4)

    def facing(value):
        return jnp.where(row == 2, pltpu.roll(value, 2, 0), jnp.where(row == 5, pltpu.roll(value, 6, 0), value))

    def gathered(value):
        paired = jnp.where(row == 0, pltpu.roll(value, 6, 0), jnp.where(row == 7, pltpu.roll(value, 2, 0), 0.0))
        return jnp.where((row < 2) | (row > 5), value + paired, 0.0)

    home = [doubled(ring_rows(c, 0)) for c in range(3)]
    edge = [facing(rows(c, 8)) for c in range(3)]
    sources = [beyond[pl.ds(c * 8, 8), :] for c in range(7)]
    zero = jnp.zeros((8, BLOCK), F32)
    ring_sums, edge_sums = [zero] * 18, [zero] * 18
    for slot, (sy, sz, x_steps) in enumerate(OFFSETS):
        shift = lane_turn(sy, sz)
        reach = reach_of(sz)
        for step in RING_STEPS:
            if step == 0 and 2 not in x_steps or step == -1 and 1 not in x_steps:
                continue
            limit = reach if step < 0 else jnp.where(twice, -100.0, reach)
            other = turn([pairs[step + 2, c] for c in range(7)], shift)
            add_visit(ring_sums, home, other, limit, shift != 0)
        if 1 in x_steps:
            limit = jnp.where(used, reach, -100.0)
            g = add_visit(edge_sums, edge, turn(sources, shift), limit, True)
            for a in range(3):
                beyond_weights[slot, a] = g[a]

    ring_sums = [value + pltpu.roll(value, 6, 0) for value in ring_sums]
    own_sums = [core_sums[s] + gathered(edge_sums[s]) for s in range(18)]

    def stresses(acc, local):
        strain_sum = [acc[6 + 3 * a + b] - local[3 + a] * acc[15 + b] for a in range(3) for b in range(3)]
        return constitutive(acc[0:6], strain_sum, local[7:13], local[13])

    own_piola, own_plastic = stresses(own_sums, [rows(c, 8) for c in range(COMPS)])
    ring_piola, _ = stresses(ring_sums, [ring_rows(c, 0) for c in range(COMPS)])
    ring_piola = [
        jnp.where(row < 2, value, jnp.where(row < 6, pltpu.roll(value, 1, 0), pltpu.roll(value, 2, 0)))
        for value in ring_piola
    ]
    for s in range(6):
        results[pl.ds((3 + s) * 8, 8), :] = own_plastic[s]
    lean = own_sums[15:18]
    force = [sum(own_piola[3 * a + b] * lean[b] for b in range(3)) for a in range(3)]
    edge_force = [zero] * 3
    for slot, (sy, sz, x_steps) in enumerate(OFFSETS):
        shift = lane_turn(sy, sz)
        rolled_piolas[slot, 0:8, :] = zero
        rolled_piolas[slot, 80:88, :] = zero
        for c, value in enumerate(turn(own_piola, shift)):
            rolled_piolas[slot, pl.ds(8 + c * 8, 8), :] = value
        for sx in x_steps:
            if (sx, sy, sz) == (0, 0, 0):
                continue
            g = [weights[slot, (sx + 2) * 3 + a] for a in range(3)]
            for a in range(3):
                for b in range(3):
                    other = rolled_piolas[slot, pl.ds(8 + (3 * a + b) * 8 + sx, 8), :]
                    force[a] = force[a] + other * g[b]
        if 1 in x_steps:
            other = turn(ring_piola, shift)
            for a in range(3):
                for b in range(3):
                    edge_force[a] = edge_force[a] + other[3 * a + b] * beyond_weights[slot, b]
    force = [force[a] + gathered(edge_force[a]) for a in range(3)]

    volume = rows(VOLUME, 8)
    for a in range(3):
        results[pl.ds(a * 8, 8), :] = volume * force[a]
    for c in range(9, 16):
        results[pl.ds(c * 8, 8), :] = zero

    chunk = lax.broadcasted_iota(jnp.int32, (COMPS, BLOCK), 1) // 32
    for bx in range(2):
        lines = [results[pl.ds(bx * 4 + x, COMPS, stride=8), :] for x in range(4)]
        for by in range(2):
            block = bx * 2 + by
            turned = [pltpu.roll(lines[x], 32 * (x - by - 1) % 128, 1) for x in range(4)]
            low = jnp.where(chunk == 0, turned[0], turned[1])
            high = jnp.where(chunk == 2, turned[2], turned[3])
            value = exact_product(jnp.where(chunk < 2, low, high), onehots[block], 0)
            lanes = pl.ds(block * BLOCK, BLOCK)
            force_ref[:, lanes] = value[0:3]
            plastic_out_ref[:, lanes] = value[3:9]


def solution(mesh):
    n_gx, n_gy = mesh.shape["gx"], mesh.shape["gy"]

    def on_device(ref_pos, disp, volume, plastic, material, pair_list, pair_count):
        count = ref_pos.shape[1]
        vmem = pl.BlockSpec(memory_space=pltpu.VMEM)
        inputs = [
            pltpu.with_memory_space_constraint(array, pltpu.HBM)
            for array in (
                ref_pos, disp, volume.reshape(1, count), plastic, material.reshape(1, count)
            )
        ]
        shared = pl.pallas_call(
            functools.partial(exchange_kernel, n_gx, n_gy),
            out_shape=(
                jax.ShapeDtypeStruct((4, 4, COMPS, BLOCK), F32),
                jax.ShapeDtypeStruct((4, BLOCK, BLOCK), jnp.bfloat16),
                jax.ShapeDtypeStruct((COMPS * 8, BLOCK), F32),
                jax.ShapeDtypeStruct((18, 8, BLOCK), F32),
                jax.ShapeDtypeStruct((25, 15, 8, BLOCK), F32),
            ),
            in_specs=[pl.BlockSpec(memory_space=pltpu.HBM)] * 5,
            out_specs=(vmem,) * 5,
            scratch_shapes=[
                pltpu.VMEM((3, count), F32),
                pltpu.VMEM((3, count), F32),
                pltpu.VMEM((1, count), F32),
                pltpu.VMEM((6, count), F32),
                pltpu.VMEM((1, count), jnp.int32),
                pltpu.VMEM((4, COMPS, BLOCK), F32),
                pltpu.VMEM((8, COMPS, BLOCK), F32),
                pltpu.VMEM((25, 72, BLOCK), F32),
                pltpu.SemaphoreType.DMA((5,)),
                pltpu.SemaphoreType.DMA((8,)),
                pltpu.SemaphoreType.DMA((8,)),
            ],
            compiler_params=pltpu.CompilerParams(
                collective_id=0, has_side_effects=True, vmem_limit_bytes=8 << 20
            ),
        )(*inputs)
        return pl.pallas_call(
            stencil_kernel,
            out_shape=(
                jax.ShapeDtypeStruct((3, count), F32),
                jax.ShapeDtypeStruct((6, count), F32),
            ),
            in_specs=[vmem] * 5,
            out_specs=(vmem, vmem),
            scratch_shapes=[
                pltpu.VMEM((COMPS * 24, BLOCK), F32),
                pltpu.VMEM((3, 7, 8, BLOCK), F32),
                pltpu.VMEM((COMPS * 8, BLOCK), F32),
                pltpu.VMEM((25, 3, 8, BLOCK), F32),
                pltpu.VMEM((25, 88, BLOCK), F32),
                pltpu.VMEM((COMPS * 8, BLOCK), F32),
            ],
            compiler_params=pltpu.CompilerParams(vmem_limit_bytes=16 << 20),
        )(*shared)

    in_specs = (
        P(None, ("gx", "gy")),
        P(None, ("gx", "gy")),
        P(("gx", "gy")),
        P(None, ("gx", "gy")),
        P(("gx", "gy")),
        P(("gx", "gy"), None, None),
        P(("gx", "gy")),
    )
    out_specs = (P(None, ("gx", "gy")), P(None, ("gx", "gy")))
    return jax.shard_map(
        on_device, mesh=mesh, in_specs=in_specs, out_specs=out_specs, check_vma=False
    )
```
